256 devices in a mesh: doc: 16 (over z_hi, x, core), vocab: 16 (over z_lo, y).
Axes of the slice: x: 4, y: 4, z: 8 (z_hi: 2, z_lo: 4; z = z_hi * 4 + z_lo), core: 2. Of those that a mesh axis runs over, the one named last changes fastest.
Arguments:
- counts: bfloat16 [1024, 512, 128], P('doc', 'vocab'), may hold values from 0.099609375 to 3
- tile_index: int32 [1024, 512], P('doc', 'vocab'), may hold values from 0 to 31
- tile_count: int32 [1024, 256], P('doc', 'vocab'), may hold values from 0 to 2
- whitening: bfloat16 [1048576, 512], P(('doc', 'vocab')), may hold values from -0.046875 to 0.046875
- factors: float32 [512, 512], replicated, may hold values from -6 to 6
Outputs:
- gradient: float32 [512, 512], replicated
The draws below stay inside these ranges and needn't reach their ends.
Inputs may be any that keep to these rules, and one draw needn't show every extreme that they name: `tile_count`: slots at or past a document block's live count carry no data. `tile_index`: tile numbers within a row block; two live slots may name the same tile.
All inputs are finite; a program needn't handle non-finite values.
Results may differ from the reference program's by a relative error of at most 0.00033.
Values may be sent and summed in bfloat16 or wider, within the bound.
No kernel may reach another device: no remote copies, remote signals or barrier semaphores. Data moves between devices by JAX's collectives and lax.ppermute only.
A program may use at most 64 MiB of HBM per device.

```python
import math
import jax
import jax.numpy as jnp
from jax import lax

K = 512
WORDS_DEV = 4096
TILE = 128
SLOTS = 2
TILES_DEV = 32
VOCAB = 1048576
DOCS = 1024
N_DOC = 16
N_VOCAB = 16


def touch_ends(result, stream_key, low, high):
    dims = result.shape
    place = [jax.random.randint(jax.random.fold_in(stream_key, axis), (), 0, dims[axis]) for axis in range(len(dims))]
    result = result.at[tuple(place)].set(low)
    longest = dims.index(max(dims))
    place[longest] = (place[longest] + 1) % dims[longest]
    return result.at[tuple(place)].set(high)


def level_of(rng, extent, cuts, smallest, largest):
    level, own = 1.0, jax.random.fold_in(rng, 6)
    for position, shards_of in cuts:
        heights = jnp.exp(jax.random.uniform(jax.random.fold_in(own, position), (shards_of,), jnp.float32, smallest / len(cuts), largest / len(cuts)))
        level = level * jnp.repeat(heights, extent[position] // shards_of).reshape([-1 if axis == position else 1 for axis in range(len(extent))])
    return level


def normal_values(stream_key, dims, deviation, reach, shards=(), dtype=jnp.bfloat16):
    drawn = jax.random.normal(stream_key, dims, jnp.float32) * deviation
    if len(shards) > 0:
        drawn = level_of(stream_key, dims, shards, -0.22, 0.18) * drawn
    return jnp.clip(drawn, min=-reach, max=reach).astype(dtype)


def setup_inputs(seed: int = 0) -> dict:
    key_list = jax.random.split(jax.random.key(seed), 6)
    return {
        "counts": jnp.clip(jnp.exp(math.log(3.0) - 3.4051113 * jax.random.uniform(key_list[0], (DOCS, N_VOCAB * N_DOC * SLOTS, TILE), jnp.float32) ** level_of(key_list[0], (DOCS, N_VOCAB * N_DOC * SLOTS, TILE), ((0, 16), (1, 16)), -0.2, 0.2)), 0.099609375, 3.0).astype(jnp.bfloat16),
        "tile_index": touch_ends(jax.random.randint(key_list[1], (DOCS, N_VOCAB * N_DOC * SLOTS), 0, TILES_DEV), jax.random.fold_in(key_list[1], 1), 0, TILES_DEV - 1).astype(jnp.int32),
        "tile_count": touch_ends(jax.random.randint(key_list[2], (DOCS, N_VOCAB * N_DOC), 0, SLOTS + 1), jax.random.fold_in(key_list[2], 1), 0, SLOTS).astype(jnp.int32),
        "whitening": normal_values(key_list[3], (VOCAB, K), (VOCAB // 64) ** -0.5, 0.046875, ((0, 256),)),
        "factors": normal_values(key_list[4], (K, K), 1.0, 6.0, (), jnp.float32),
    }


penalty = 0.25

def reference(counts, tile_index, tile_count, whitening, factors):
    block_total = N_DOC * N_VOCAB
    tiles_block = WORDS_DEV // TILE
    count_blocks = counts.reshape(DOCS, N_VOCAB, N_DOC, SLOTS, TILE).transpose(2, 1, 0, 3, 4)
    count_blocks = count_blocks.reshape(block_total, DOCS, SLOTS, TILE)
    index_blocks = tile_index.reshape(DOCS, N_VOCAB, N_DOC, SLOTS).transpose(2, 1, 0, 3)
    index_blocks = index_blocks.reshape(block_total, DOCS, SLOTS)
    live_blocks = tile_count.reshape(DOCS, N_VOCAB, N_DOC).transpose(2, 1, 0).reshape(block_total, DOCS)
    weight_blocks = whitening.reshape(block_total, WORDS_DEV, K)
    slot_iota = lax.broadcasted_iota(jnp.int32, (1, SLOTS), 1)
    tile_iota = lax.broadcasted_iota(jnp.int32, (1, 1, tiles_block), 2)

    def one_block(running, inputs):
        block_counts, block_index, block_live, block_weight = inputs
        live_slot = slot_iota < block_live[:, None]
        onehot = ((block_index[:, :, None] == tile_iota) & live_slot[:, :, None]).astype(jnp.float32)
        dense_block = jnp.einsum('dst,dsw->dtw', onehot, block_counts.astype(jnp.float32))
        dense_block = dense_block.astype(jnp.bfloat16).reshape(DOCS, WORDS_DEV)
        return (running + jnp.dot(dense_block, block_weight, preferred_element_type=jnp.float32), None)
    start_value = jnp.zeros((DOCS, K), jnp.float32)
    projected, unused = lax.scan(one_block, start_value, (count_blocks, index_blocks, live_blocks, weight_blocks))
    highest = lax.Precision.HIGHEST
    scores = jnp.dot(projected, factors, precision=highest) / math.sqrt(K)
    moment = jnp.dot(projected.T, scores * scores, precision=highest) / DOCS
    gram_matrix = jnp.dot(factors.T, factors, precision=highest) / K
    return moment - penalty * jnp.dot(factors, gram_matrix * gram_matrix, precision=highest)
```

```python
import math

import jax
import jax.numpy as jnp
from jax import lax
from jax.sharding import Mesh, PartitionSpec as P

penalty = 0.25
term_scale = 256.0
total_scale = 4.0
HIGH = lax.Precision.HIGH


def project_rows(tile_rows, slot_tile, whitening):
    rows, _, tile_width = tile_rows.shape
    tiles_block = whitening.shape[0] // tile_width
    tile_iota = lax.broadcasted_iota(jnp.int32, (1, 1, tiles_block), 2)
    onehot = (slot_tile[:, :, None] == tile_iota).astype(jnp.bfloat16)
    dense_block = jnp.einsum("dst,dsw->dtw", onehot, tile_rows, preferred_element_type=jnp.float32)
    dense_block = dense_block.astype(jnp.bfloat16).reshape(rows, tiles_block * tile_width)
    return jnp.dot(dense_block, whitening, preferred_element_type=jnp.float32)


def to_half(values, scale):
    return (values * scale).astype(jnp.float16)


def from_half(values, scale):
    return values.astype(jnp.float32) * (1.0 / scale)


def shards(counts, tile_index, tile_count, whitening, factors):
    doc_axes = ("zh", "x", "c")
    doc_devices = lax.axis_size(doc_axes)
    doc_local = counts.shape[0]
    slot_count = counts.shape[1] // doc_devices
    tile_width = counts.shape[2]
    topics = whitening.shape[1]
    doc_total = doc_local * doc_devices
    slot_iota = lax.broadcasted_iota(jnp.int32, (1, 1, slot_count), 2)
    live_slot = slot_iota < tile_count[:, :, None]
    marked = jnp.where(live_slot, tile_index.reshape(doc_local, doc_devices, slot_count), -1)
    blocks = counts.reshape(doc_local, doc_devices, slot_count, tile_width)
    moved_index = lax.all_to_all(marked, doc_axes, split_axis=1, concat_axis=0, tiled=True)
    moved_counts = lax.all_to_all(blocks, doc_axes, split_axis=1, concat_axis=0, tiled=True)
    tile_rows = moved_counts.reshape(doc_total, slot_count, tile_width)
    slot_tile = moved_index.reshape(doc_total, slot_count)
    terms = project_rows(tile_rows, slot_tile, whitening)

    core = lax.axis_index("c")
    half = doc_total // 2
    swap = [(0, 1), (1, 0)]
    away = lax.dynamic_slice_in_dim(terms, (1 - core) * half, half, 0)
    kept = lax.dynamic_slice_in_dim(terms, core * half, half, 0)
    kept = kept + from_half(lax.ppermute(to_half(away, term_scale), "c", swap), term_scale)

    plane = lax.axis_size(("x", "y"))
    column = lax.axis_size(("zh", "zl"))
    part = half // plane
    sent = to_half(kept, term_scale).reshape(plane, part, topics)
    got = lax.all_to_all(sent, ("x", "y"), 0, 0, tiled=True)
    plane_sum = jnp.sum(got.astype(jnp.float32), axis=0) * (1.0 / term_scale)
    sent = jnp.broadcast_to(to_half(plane_sum, total_scale)[None], (column, part, topics))
    got = lax.all_to_all(sent, ("zh", "zl"), 0, 0, tiled=True)
    total = jnp.sum(got.astype(jnp.float32), axis=0) * (1.0 / total_scale)
    sent = jnp.broadcast_to(to_half(total, total_scale)[None], (plane, part, topics))
    got = lax.all_to_all(sent, ("x", "y"), 0, 0, tiled=True)
    projected = from_half(got.reshape(half, topics), total_scale)

    scores = jnp.dot(projected, factors, precision=HIGH) * (1.0 / math.sqrt(topics))
    moment = jnp.dot(projected.T, scores * scores, precision=HIGH)
    moment = (moment + lax.ppermute(moment, "c", swap)) / doc_total
    gram_matrix = jnp.dot(factors.T, factors, precision=HIGH) / topics
    return moment - penalty * jnp.dot(factors, gram_matrix * gram_matrix, precision=HIGH)


def solution(mesh):
    fine = Mesh(mesh.devices.reshape(2, 4, 2, 4, 4), ("zh", "x", "c", "zl", "y"))
    doc, vocab = ("zh", "x", "c"), ("zl", "y")
    in_specs = (P(doc, vocab, None), P(doc, vocab), P(doc, vocab), P(doc + vocab, None), P())
    return jax.shard_map(shards, mesh=fine, in_specs=in_specs, out_specs=P(), check_vma=False)
```

```python
import functools
import math

import jax
import jax.numpy as jnp
from jax import lax
from jax.experimental import pallas as pl
from jax.experimental.pallas import tpu as pltpu
from jax.sharding import Mesh, PartitionSpec as P

penalty = 0.25
term_scale = 256.0
total_scale = 4.0
HIGH = lax.Precision.HIGH
STEPS = 4


def pack_kernel(index_ref, live_ref, counts_ref, out_ref, sems):
    targets, units, group, width = out_ref.shape
    chips = targets // 2
    docs = units - 2
    copies = []
    for chip in range(chips):
        for core in range(2):
            target = chip * 2 + core
            copy = pltpu.make_async_copy(
                counts_ref.at[pl.ds(core * docs, docs), chip],
                out_ref.at[target, pl.ds(0, docs)],
                sems.at[target],
            )
            copy.start()
            copies.append(copy)
    slots = group // 2
    marked = []
    for lane in range(group):
        tile = index_ref[pl.ds(lane, chips, stride=group), :]
        live = live_ref[pl.ds(lane // slots, chips, stride=2), :]
        marked.append(jnp.where(lane % slots < live, tile, -1).astype(jnp.float32))
    for core in range(2):
        rows = jnp.concatenate([m[:, core * docs:(core + 1) * docs] for m in marked], axis=1)
        for chip in range(chips):
            row = jnp.broadcast_to(rows[chip:chip + 1, :], (2 * group, width))
            out_ref[chip * 2 + core, docs:docs + 2] = row.reshape(2, group, width).astype(out_ref.dtype)
    for copy in copies:
        copy.wait()


def project_kernel(core_ref, moved_ref, own_ref, other_ref, early_ref, out_ref,
                   weights, spread, values, tiles, sems):
    sources, rows, width = moved_ref.shape
    group = 4
    data = rows - 2 * group
    docs = data // group
    depth = own_ref.shape[0] // STEPS
    copies = []
    for step in range(2 * STEPS):
        source = own_ref if step < STEPS else other_ref
        copy = pltpu.make_async_copy(
            source.at[pl.ds((step % STEPS) * depth, depth)], weights.at[step], sems.at[step])
        copy.start()
        copies.append(copy)

    sub = lax.broadcasted_iota(jnp.int32, (8, width), 0)
    halves = []
    for base in range(0, sources, 8):
        part = jnp.zeros((8, width), jnp.float32)
        for k in range(8):
            part = jnp.where(sub == k, moved_ref[base + k, data:data + 8, :].astype(jnp.float32), part)
        halves.append(part)
    halves.append(jnp.zeros((width - sources, width), jnp.float32))
    index = jnp.transpose(jnp.concatenate(halves, axis=0))
    for k in range(sources):
        spread[k * data:(k + 1) * data, :] = moved_ref[k, :data, :].astype(jnp.float32)
    total = sources * docs
    for block in range(2):
        where = []
        for slot in range(2):
            lane = block * 2 + slot
            where.append(jnp.concatenate(
                [jnp.broadcast_to(index[lane * docs:(lane + 1) * docs, k:k + 1], (docs, width))
                 for k in range(sources)], axis=0))
        first = spread[pl.ds(block * 2, total, stride=group), :]
        second = spread[pl.ds(block * 2 + 1, total, stride=group), :]
        first = jnp.where(where[0] == where[1], first + second, first)
        values[block * 2] = first.astype(jnp.bfloat16)
        values[block * 2 + 1] = second.astype(jnp.bfloat16)
        tiles[block * 2] = where[0].astype(jnp.bfloat16)
        tiles[block * 2 + 1] = where[1].astype(jnp.bfloat16)

    core = core_ref[0]
    tiles_step = depth // width

    def one_step(step):
        block = jnp.where(step < STEPS, core, 1 - core)
        base = (lax.rem(step, STEPS) * tiles_step).astype(jnp.float32)
        base = jnp.full((1, width), base, jnp.float32).astype(jnp.bfloat16)
        tile_a = tiles[block * 2] - base
        tile_b = tiles[block * 2 + 1] - base
        value_a = values[block * 2]
        value_b = values[block * 2 + 1]
        none = jnp.zeros_like(value_a)
        parts = []
        for t in range(tiles_step):
            mark = jnp.full((1, width), t, jnp.bfloat16)
            parts.append(jnp.where(tile_a == mark, value_a, jnp.where(tile_b == mark, value_b, none)))
        dense = jnp.concatenate(parts, axis=1)
        pltpu.make_async_copy(own_ref.at[pl.ds(0, depth)], weights.at[step], sems.at[step]).wait()
        return jnp.dot(dense, weights[step], preferred_element_type=jnp.float32)

    out_ref[...] = one_step(jnp.int32(0))

    @pl.loop(1, 2 * STEPS)
    def _(step):
        out_ref[...] += one_step(step)


def to_half(values, scale):
    return (values * scale).astype(jnp.float16)


def from_half(values, scale):
    return values.astype(jnp.float32) * (1.0 / scale)


def shards(counts, tile_index, tile_count, whitening, factors):
    doc_axes = ("zh", "x", "c")
    doc_devices = lax.axis_size(doc_axes)
    chips = doc_devices // 2
    doc_local = counts.shape[0]
    slots = counts.shape[1] // doc_devices
    width = counts.shape[2]
    topics = whitening.shape[1]
    half = doc_local * chips
    group = 2 * slots
    swap = [(0, 1), (1, 0)]
    vmem = pl.BlockSpec(memory_space=pltpu.VMEM)
    anywhere = pl.BlockSpec(memory_space=pl.ANY)

    other = lax.ppermute(whitening, "c", swap)
    units = doc_local // 2 + 2
    packed = pl.pallas_call(
        pack_kernel,
        out_shape=jax.ShapeDtypeStruct((doc_devices, units, group, width), jnp.bfloat16),
        in_specs=[vmem, vmem, anywhere],
        out_specs=vmem,
        scratch_shapes=[pltpu.SemaphoreType.DMA((doc_devices,))],
        compiler_params=pltpu.CompilerParams(vmem_limit_bytes=8 << 20),
        cost_estimate=pl.CostEstimate(flops=1 << 20, bytes_accessed=2 << 20, transcendentals=0),
        name="pack",
    )(tile_index.T, tile_count.T, counts.reshape(doc_local, chips, group, width))
    moved = lax.all_to_all(packed, doc_axes, 0, 0, tiled=True)
    moved = moved.reshape(doc_devices, units * group, width)

    gram_matrix = jnp.dot(factors.T, factors, precision=HIGH) / topics
    early = penalty * jnp.dot(factors, gram_matrix * gram_matrix, precision=HIGH)
    core = lax.axis_index("c")
    depth = whitening.shape[0] // STEPS
    terms = pl.pallas_call(
        project_kernel,
        out_shape=jax.ShapeDtypeStruct((half, topics), jnp.float32),
        in_specs=[pl.BlockSpec(memory_space=pltpu.SMEM), vmem, anywhere, anywhere, anywhere],
        out_specs=vmem,
        scratch_shapes=[
            pltpu.VMEM((2 * STEPS, depth, topics), jnp.bfloat16),
            pltpu.VMEM((half * group, width), jnp.float32),
            pltpu.VMEM((group, half, width), jnp.bfloat16),
            pltpu.VMEM((group, half, width), jnp.bfloat16),
            pltpu.SemaphoreType.DMA((2 * STEPS,)),
        ],
        compiler_params=pltpu.CompilerParams(vmem_limit_bytes=24 << 20),
        cost_estimate=pl.CostEstimate(
            flops=4 * half * whitening.shape[0] * topics, bytes_accessed=12 << 20, transcendentals=0),
        name="project",
    )(core.astype(jnp.int32).reshape(1), moved, whitening, other, early)

    plane_axes, column_axes = ("y", "x"), ("zh", "zl")
    plane = lax.axis_size(plane_axes)
    column = lax.axis_size(column_axes)
    part = half // plane
    sent = to_half(terms, term_scale).reshape(plane, part, topics)
    got = lax.all_to_all(sent, plane_axes, 0, 0, tiled=True)
    plane_sum = jnp.sum(got.astype(jnp.float32), axis=0) * (1.0 / term_scale)
    sent = jnp.broadcast_to(to_half(plane_sum, total_scale)[None], (column, part, topics))
    got = lax.all_to_all(sent, column_axes, 0, 0, tiled=True)
    total = jnp.sum(got.astype(jnp.float32), axis=0) * (1.0 / total_scale)
    sent = jnp.broadcast_to(to_half(total, total_scale)[None], (plane, part, topics))
    got = lax.all_to_all(sent, plane_axes, 0, 0, tiled=True)
    projected = from_half(got.reshape(half, topics), total_scale)

    scores = jnp.dot(projected, factors, precision=HIGH) * (1.0 / math.sqrt(topics))
    moment = jnp.dot(projected.T, scores * scores, precision=HIGH)
    return (moment + lax.ppermute(moment, "c", swap)) * (1.0 / (2 * half)) - early


def solution(mesh):
    fine = Mesh(mesh.devices.reshape(2, 4, 2, 4, 4), ("zh", "x", "c", "zl", "y"))
    doc, vocab = ("zh", "x", "c"), ("zl", "y")
    in_specs = (P(doc, vocab, None), P(doc, vocab), P(doc, vocab), P(doc + vocab, None), P())
    return jax.shard_map(shards, mesh=fine, in_specs=in_specs, out_specs=P(), check_vma=False)
```

```python
import functools
import math

import jax
import jax.numpy as jnp
from jax import lax
from jax.experimental import pallas as pl
from jax.experimental.pallas import tpu as pltpu
from jax.sharding import Mesh, PartitionSpec as P

penalty = 0.25
term_scale = 256.0
total_scale = 4.0
HIGH = lax.Precision.HIGH
STEPS = 4


def pack_kernel(index_ref, live_ref, counts_ref, out_ref, sems):
    targets, units, group, width = out_ref.shape
    chips = targets // 2
    docs = units - 2
    copies = []
    for chip in range(chips):
        for core in range(2):
            target = chip * 2 + core
            copy = pltpu.make_async_copy(
                counts_ref.at[pl.ds(core * docs, docs), chip],
                out_ref.at[target, pl.ds(0, docs)],
                sems.at[target],
            )
            copy.start()
            copies.append(copy)
    slots = group // 2
    marked = []
    for lane in range(group):
        tile = index_ref[pl.ds(lane, chips, stride=group), :]
        live = live_ref[pl.ds(lane // slots, chips, stride=2), :]
        marked.append(jnp.where(lane % slots < live, tile, -1).astype(jnp.float32))
    for core in range(2):
        rows = jnp.concatenate([m[:, core * docs:(core + 1) * docs] for m in marked], axis=1)
        for chip in range(chips):
            row = jnp.broadcast_to(rows[chip:chip + 1, :], (2 * group, width))
            out_ref[chip * 2 + core, docs:docs + 2] = row.reshape(2, group, width).astype(out_ref.dtype)
    for copy in copies:
        copy.wait()


def project_kernel(core_ref, moved_ref, own_ref, other_ref, early_ref, out_ref,
                   weights, spread, values, tiles, sems):
    sources, rows, width = moved_ref.shape
    group = 4
    data = rows - 2 * group
    docs = data // group
    depth = own_ref.shape[0] // STEPS
    copies = []
    for step in range(2 * STEPS):
        source = own_ref if step < STEPS else other_ref
        copy = pltpu.make_async_copy(
            source.at[pl.ds((step % STEPS) * depth, depth)], weights.at[step], sems.at[step])
        copy.start()
        copies.append(copy)

    sub = lax.broadcasted_iota(jnp.int32, (8, width), 0)
    halves = []
    for base in range(0, sources, 8):
        part = jnp.zeros((8, width), jnp.float32)
        for k in range(8):
            part = jnp.where(sub == k, moved_ref[base + k, data:data + 8, :].astype(jnp.float32), part)
        halves.append(part)
    halves.append(jnp.zeros((width - sources, width), jnp.float32))
    index = jnp.transpose(jnp.concatenate(halves, axis=0))
    for k in range(sources):
        spread[k * data:(k + 1) * data, :] = moved_ref[k, :data, :].astype(jnp.float32)
    total = sources * docs
    for block in range(2):
        where = []
        for slot in range(2):
            lane = block * 2 + slot
            where.append(jnp.concatenate(
                [jnp.broadcast_to(index[lane * docs:(lane + 1) * docs, k:k + 1], (docs, width))
                 for k in range(sources)], axis=0))
        first = spread[pl.ds(block * 2, total, stride=group), :]
        second = spread[pl.ds(block * 2 + 1, total, stride=group), :]
        first = jnp.where(where[0] == where[1], first + second, first)
        values[block * 2] = first.astype(jnp.bfloat16)
        values[block * 2 + 1] = second.astype(jnp.bfloat16)
        tiles[block * 2] = where[0].astype(jnp.bfloat16)
        tiles[block * 2 + 1] = where[1].astype(jnp.bfloat16)

    core = core_ref[0]
    tiles_step = depth // width

    out_ref[...] = jnp.zeros_like(out_ref)

    @pl.loop(0, 2 * STEPS)
    def _(step):
        pltpu.make_async_copy(own_ref.at[pl.ds(0, depth)], weights.at[step], sems.at[step]).wait()
        block = jnp.where(step < STEPS, core, 1 - core)
        base = (lax.rem(step, STEPS) * tiles_step).astype(jnp.float32)
        total = out_ref[...]
        for chunk in range(tiles_step // 2):
            parts = []
            for t in (2 * chunk, 2 * chunk + 1):
                mark = jnp.full((1, width), base + t, jnp.float32).astype(jnp.bfloat16)
                parts.append(jnp.where(
                    tiles[block * 2] == mark, values[block * 2],
                    jnp.where(tiles[block * 2 + 1] == mark, values[block * 2 + 1], jnp.zeros((), jnp.bfloat16))))
            dense = jnp.concatenate(parts, axis=1)
            total = total + jnp.dot(
                dense, weights[step, 2 * chunk * width:2 * (chunk + 1) * width, :],
                preferred_element_type=jnp.float32)
        out_ref[...] = total


def to_half(values, scale):
    return (values * scale).astype(jnp.float16)


def from_half(values, scale):
    return values.astype(jnp.float32) * (1.0 / scale)


def shards(counts, tile_index, tile_count, whitening, factors):
    doc_axes = ("zh", "x", "c")
    doc_devices = lax.axis_size(doc_axes)
    chips = doc_devices // 2
    doc_local = counts.shape[0]
    slots = counts.shape[1] // doc_devices
    width = counts.shape[2]
    topics = whitening.shape[1]
    half = doc_local * chips
    group = 2 * slots
    swap = [(0, 1), (1, 0)]
    vmem = pl.BlockSpec(memory_space=pltpu.VMEM)
    anywhere = pl.BlockSpec(memory_space=pl.ANY)
    hbm = pl.BlockSpec(memory_space=pltpu.HBM)

    other = lax.ppermute(whitening, "c", swap)
    units = doc_local // 2 + 2
    packed = pl.pallas_call(
        pack_kernel,
        out_shape=jax.ShapeDtypeStruct((doc_devices, units, group, width), jnp.bfloat16),
        in_specs=[vmem, vmem, anywhere],
        out_specs=vmem,
        scratch_shapes=[pltpu.SemaphoreType.DMA((doc_devices,))],
        compiler_params=pltpu.CompilerParams(vmem_limit_bytes=61 << 20),
        cost_estimate=pl.CostEstimate(flops=1 << 20, bytes_accessed=2 << 20, transcendentals=0),
        name="pack",
    )(tile_index.T, tile_count.T, counts.reshape(doc_local, chips, group, width))
    moved = lax.all_to_all(packed, doc_axes, 0, 0, tiled=True)
    moved = moved.reshape(doc_devices, units * group, width)

    gram_matrix = jnp.dot(factors.T, factors, precision=HIGH) / topics
    early = penalty * jnp.dot(factors, gram_matrix * gram_matrix, precision=HIGH)
    core = lax.axis_index("c")
    depth = whitening.shape[0] // STEPS
    terms = pl.pallas_call(
        project_kernel,
        out_shape=jax.ShapeDtypeStruct((half, topics), jnp.float32),
        in_specs=[pl.BlockSpec(memory_space=pltpu.SMEM), vmem, hbm, hbm, anywhere],
        out_specs=vmem,
        scratch_shapes=[
            pltpu.VMEM((2 * STEPS, depth, topics), jnp.bfloat16),
            pltpu.VMEM((half * group, width), jnp.float32),
            pltpu.VMEM((group, half, width), jnp.bfloat16),
            pltpu.VMEM((group, half, width), jnp.bfloat16),
            pltpu.SemaphoreType.DMA((2 * STEPS,)),
        ],
        compiler_params=pltpu.CompilerParams(vmem_limit_bytes=50 << 20),
        cost_estimate=pl.CostEstimate(
            flops=4 * half * whitening.shape[0] * topics, bytes_accessed=12 << 20, transcendentals=0),
        name="project",
    )(core.astype(jnp.int32).reshape(1), moved, whitening, other, early)

    plane_axes, column_axes = ("y", "x"), ("zh", "zl")
    plane = lax.axis_size(plane_axes)
    column = lax.axis_size(column_axes)
    part = half // plane
    sent = to_half(terms, term_scale).reshape(plane, part, topics)
    got = lax.all_to_all(sent, plane_axes, 0, 0, tiled=True)
    plane_sum = jnp.sum(got.astype(jnp.float32), axis=0) * (1.0 / term_scale)
    sent = jnp.broadcast_to(to_half(plane_sum, total_scale)[None], (column, part, topics))
    got = lax.all_to_all(sent, column_axes, 0, 0, tiled=True)
    total = jnp.sum(got.astype(jnp.float32), axis=0) * (1.0 / total_scale)
    sent = jnp.broadcast_to(to_half(total, total_scale)[None], (plane, part, topics))
    got = lax.all_to_all(sent, plane_axes, 0, 0, tiled=True)
    projected = from_half(got.reshape(half, topics), total_scale)

    scores = jnp.dot(projected, factors, precision=HIGH) * (1.0 / math.sqrt(topics))
    moment = jnp.dot(projected.T, scores * scores, precision=HIGH)
    return (moment + lax.ppermute(moment, "c", swap)) * (1.0 / (2 * half)) - early


def solution(mesh):
    fine = Mesh(mesh.devices.reshape(2, 4, 2, 4, 4), ("zh", "x", "c", "zl", "y"))
    doc, vocab = ("zh", "x", "c"), ("zl", "y")
    in_specs = (P(doc, vocab, None), P(doc, vocab), P(doc, vocab), P(doc + vocab, None), P())
    return jax.shard_map(shards, mesh=fine, in_specs=in_specs, out_specs=P(), check_vma=False)
```

```python
import math

import jax
import jax.numpy as jnp
from jax import lax
from jax.experimental import pallas as pl
from jax.experimental.pallas import tpu as pltpu
from jax.sharding import Mesh, PartitionSpec as P


penalty = 0.25
term_scale = 256.0
total_scale = 4.0
HIGH = lax.Precision.HIGH
STEPS = 4
PROJECT_VMEM = 50 << 20


def pack_kernel(side_ref, index_ref, live_ref, counts_ref, near_ref, far_ref, sems):
    targets, units, group, width = near_ref.shape
    chips = targets // 2
    docs = units - 2
    side = side_ref[0]
    copies = []
    for far, out_ref in ((1, far_ref), (0, near_ref)):
        first = jnp.where(far == 1, 1 - side, side) * chips
        for chip in range(chips):
            for core in range(2):
                target = chip * 2 + core
                copy = pltpu.make_async_copy(
                    counts_ref.at[pl.ds(core * docs, docs), first + chip],
                    out_ref.at[target, pl.ds(0, docs)],
                    sems.at[far * targets + target],
                )
                copy.start()
                copies.append(copy)
    slots = group // 2
    marked = []
    for lane in range(group):
        tile = index_ref[pl.ds(lane, 2 * chips, stride=group), :]
        live = live_ref[pl.ds(lane // slots, 2 * chips, stride=2), :]
        marked.append(jnp.where(lane % slots < live, tile, -1).astype(jnp.float32))
    for core in range(2):
        rows = jnp.concatenate([m[:, core * docs:(core + 1) * docs] for m in marked], axis=1)
        for chip in range(chips):
            low, high = rows[chip:chip + 1, :], rows[chips + chip:chips + chip + 1, :]
            near = jnp.where(side == 0, low, high)
            far = jnp.where(side == 0, high, low)
            for row, out_ref in ((near, near_ref), (far, far_ref)):
                row = jnp.broadcast_to(row, (2 * group, width))
                out_ref[chip * 2 + core, docs:docs + 2] = row.reshape(2, group, width).astype(out_ref.dtype)
    for copy in copies:
        copy.wait()


def project_kernel(core_ref, moved_ref, own_ref, other_ref, early_ref, out_ref,
                   weights, spread, values, tiles, sems):
    sources, rows, width = moved_ref.shape
    group = 4
    data = rows - 2 * group
    docs = data // group
    depth = own_ref.shape[0] // STEPS
    for step in range(2 * STEPS):
        source = own_ref if step < STEPS else other_ref
        copy = pltpu.make_async_copy(
            source.at[pl.ds((step % STEPS) * depth, depth)], weights.at[step], sems.at[step])
        copy.start()

    sub = lax.broadcasted_iota(jnp.int32, (8, width), 0)
    halves = []
    for base in range(0, sources, 8):
        part = jnp.zeros((8, width), jnp.float32)
        for k in range(8):
            part = jnp.where(sub == k, moved_ref[base + k, data:data + 8, :].astype(jnp.float32), part)
        halves.append(part)
    halves.append(jnp.zeros((width - sources, width), jnp.float32))
    index = jnp.transpose(jnp.concatenate(halves, axis=0))
    for k in range(sources):
        spread[k * data:(k + 1) * data, :] = moved_ref[k, :data, :].astype(jnp.float32)
    total = sources * docs
    for block in range(2):
        where = []
        for slot in range(2):
            lane = block * 2 + slot
            where.append(jnp.concatenate(
                [jnp.broadcast_to(index[lane * docs:(lane + 1) * docs, k:k + 1], (docs, width))
                 for k in range(sources)], axis=0))
        first = spread[pl.ds(block * 2, total, stride=group), :]
        second = spread[pl.ds(block * 2 + 1, total, stride=group), :]
        first = jnp.where(where[0] == where[1], first + second, first)
        values[block * 2] = first.astype(jnp.bfloat16)
        values[block * 2 + 1] = second.astype(jnp.bfloat16)
        tiles[block * 2] = where[0].astype(jnp.bfloat16)
        tiles[block * 2 + 1] = where[1].astype(jnp.bfloat16)

    core = core_ref[0]
    tiles_step = depth // width

    out_ref[...] = jnp.zeros_like(out_ref)

    @pl.loop(0, 2 * STEPS)
    def _(step):
        pltpu.make_async_copy(own_ref.at[pl.ds(0, depth)], weights.at[step], sems.at[step]).wait()
        block = jnp.where(step < STEPS, core, 1 - core)
        base = (lax.rem(step, STEPS) * tiles_step).astype(jnp.float32)
        total = out_ref[...]
        for chunk in range(tiles_step // 2):
            parts = []
            for t in (2 * chunk, 2 * chunk + 1):
                mark = jnp.full((1, width), base + t, jnp.float32).astype(jnp.bfloat16)
                parts.append(jnp.where(
                    tiles[block * 2] == mark, values[block * 2],
                    jnp.where(tiles[block * 2 + 1] == mark, values[block * 2 + 1], jnp.zeros((), jnp.bfloat16))))
            dense = jnp.concatenate(parts, axis=1)
            total = total + jnp.dot(
                dense, weights[step, 2 * chunk * width:2 * (chunk + 1) * width, :],
                preferred_element_type=jnp.float32)
        out_ref[...] = total


def to_half(values, scale):
    return (values * scale).astype(jnp.float16)


def from_half(values, scale):
    return values.astype(jnp.float32) * (1.0 / scale)


def shards(counts, tile_index, tile_count, whitening, factors):
    doc_axes = ("zh", "x", "c")
    doc_devices = lax.axis_size(doc_axes)
    chips = doc_devices // 2
    doc_local = counts.shape[0]
    slots = counts.shape[1] // doc_devices
    width = counts.shape[2]
    topics = whitening.shape[1]
    half = doc_local * chips
    group = 2 * slots
    swap = [(0, 1), (1, 0)]
    vmem = pl.BlockSpec(memory_space=pltpu.VMEM)
    anywhere = pl.BlockSpec(memory_space=pl.ANY)

    side = lax.axis_index("zh").astype(jnp.int32)
    core = lax.axis_index("c").astype(jnp.int32)
    cross_axes = ("x", "c")
    targets = lax.axis_size(cross_axes)
    units = doc_local // 2 + 2
    packed = jax.ShapeDtypeStruct((targets, units, group, width), jnp.bfloat16)
    near, far = pl.pallas_call(
        pack_kernel,
        out_shape=(packed, packed),
        in_specs=[pl.BlockSpec(memory_space=pltpu.SMEM), vmem, vmem, anywhere],
        out_specs=(vmem, vmem),
        scratch_shapes=[pltpu.SemaphoreType.DMA((2 * targets,))],
        compiler_params=pltpu.CompilerParams(vmem_limit_bytes=61 << 20),
        cost_estimate=pl.CostEstimate(flops=1 << 20, bytes_accessed=2 << 20, transcendentals=0),
        name="pack",
    )(side.reshape(1), tile_index.T, tile_count.T, counts.reshape(doc_local, chips, group, width))
    far = lax.ppermute(far, "zh", swap)
    other = lax.ppermute(whitening, "c", swap)
    near = lax.all_to_all(near, cross_axes, 0, 0, tiled=True)
    far = lax.all_to_all(far, cross_axes, 0, 0, tiled=True)

    gram_matrix = jnp.dot(factors.T, factors, precision=HIGH) / topics
    early = penalty * jnp.dot(factors, gram_matrix * gram_matrix, precision=HIGH)
    depth = whitening.shape[0] // STEPS
    quarter = half // 2

    def project(moved, after):
        return pl.pallas_call(
            project_kernel,
            out_shape=jax.ShapeDtypeStruct((quarter, topics), jnp.float32),
            in_specs=[pl.BlockSpec(memory_space=pltpu.SMEM), vmem, anywhere, anywhere, anywhere],
            out_specs=vmem,
            scratch_shapes=[
                pltpu.VMEM((2 * STEPS, depth, topics), jnp.bfloat16),
                pltpu.VMEM((quarter * group, width), jnp.float32),
                pltpu.VMEM((group, quarter, width), jnp.bfloat16),
                pltpu.VMEM((group, quarter, width), jnp.bfloat16),
                pltpu.SemaphoreType.DMA((2 * STEPS,)),
            ],
            compiler_params=pltpu.CompilerParams(vmem_limit_bytes=PROJECT_VMEM),
            cost_estimate=pl.CostEstimate(
                flops=4 * quarter * whitening.shape[0] * topics, bytes_accessed=10 << 20, transcendentals=0),
            name="project",
        )(core.reshape(1), moved.reshape(targets, units * group, width), whitening, other, after)

    near_terms = project(near, early)
    far_terms = project(far, near_terms)
    terms = jnp.concatenate([
        jnp.where(side == 0, near_terms, far_terms), jnp.where(side == 0, far_terms, near_terms)], axis=0)

    plane_axes, column_axes = ("y", "x"), ("zh", "zl")
    plane = lax.axis_size(plane_axes)
    column = lax.axis_size(column_axes)
    part = half // plane
    sent = to_half(terms, term_scale).reshape(plane, part, topics)
    got = lax.all_to_all(sent, plane_axes, 0, 0, tiled=True)
    plane_sum = jnp.sum(got.astype(jnp.float32), axis=0) * (1.0 / term_scale)
    sent = jnp.broadcast_to(to_half(plane_sum, total_scale)[None], (column, part, topics))
    got = lax.all_to_all(sent, column_axes, 0, 0, tiled=True)
    total = jnp.sum(got.astype(jnp.float32), axis=0) * (1.0 / total_scale)
    sent = jnp.broadcast_to(to_half(total, total_scale)[None], (plane, part, topics))
    got = lax.all_to_all(sent, plane_axes, 0, 0, tiled=True)
    projected = from_half(got.reshape(half, topics), total_scale)

    scores = jnp.dot(projected, factors, precision=HIGH) * (1.0 / math.sqrt(topics))
    moment = jnp.dot(projected.T, scores * scores, precision=HIGH)
    return (moment + lax.ppermute(moment, "c", swap)) * (1.0 / (2 * half)) - early


def solution(mesh):
    fine = Mesh(mesh.devices.reshape(2, 4, 2, 4, 4), ("zh", "x", "c", "zl", "y"))
    doc, vocab = ("zh", "x", "c"), ("zl", "y")
    in_specs = (P(doc, vocab, None), P(doc, vocab), P(doc, vocab), P(doc + vocab, None), P())
    return jax.shard_map(shards, mesh=fine, in_specs=in_specs, out_specs=P(), check_vma=False)
```

```python
import math

import jax
import jax.numpy as jnp
from jax import lax
from jax.experimental import pallas as pl
from jax.experimental.pallas import tpu as pltpu
from jax.sharding import Mesh, PartitionSpec as P


penalty = 0.25
term_scale = 256.0
total_scale = 4.0
HIGH = lax.Precision.HIGH
STEPS = 4
PROJECT_VMEM = 50 << 20


def pack_kernel(side_ref, index_ref, live_ref, counts_ref, near_ref, far_ref, sems):
    targets, units, group, width = near_ref.shape
    chips = targets // 2
    docs = units - 2
    side = side_ref[0]
    copies = []
    for far, out_ref in ((1, far_ref), (0, near_ref)):
        first = jnp.where(far == 1, 1 - side, side) * chips
        for chip in range(chips):
            for core in range(2):
                target = chip * 2 + core
                copy = pltpu.make_async_copy(
                    counts_ref.at[pl.ds(core * docs, docs), first + chip],
                    out_ref.at[target, pl.ds(0, docs)],
                    sems.at[far * targets + target],
                )
                copy.start()
                copies.append(copy)
    slots = group // 2
    marked = []
    for lane in range(group):
        tile = index_ref[pl.ds(lane, 2 * chips, stride=group), :]
        live = live_ref[pl.ds(lane // slots, 2 * chips, stride=2), :]
        marked.append(jnp.where(lane % slots < live, tile, -1).astype(jnp.float32))
    for core in range(2):
        rows = jnp.concatenate([m[:, core * docs:(core + 1) * docs] for m in marked], axis=1)
        for chip in range(chips):
            low, high = rows[chip:chip + 1, :], rows[chips + chip:chips + chip + 1, :]
            near = jnp.where(side == 0, low, high)
            far = jnp.where(side == 0, high, low)
            for row, out_ref in ((near, near_ref), (far, far_ref)):
                row = jnp.broadcast_to(row, (2 * group, width))
                out_ref[chip * 2 + core, docs:docs + 2] = row.reshape(2, group, width).astype(out_ref.dtype)
    for copy in copies:
        copy.wait()


def project_kernel(core_ref, moved_ref, own_ref, other_ref, early_ref, out_ref,
                   weights, spread, values, tiles, sems):
    sources, rows, width = moved_ref.shape
    group = 4
    data = rows - 2 * group
    docs = data // group
    depth = own_ref.shape[0] // STEPS
    for step in range(2 * STEPS):
        source = own_ref if step < STEPS else other_ref
        copy = pltpu.make_async_copy(
            source.at[pl.ds((step % STEPS) * depth, depth)], weights.at[step], sems.at[step])
        copy.start()

    sub = lax.broadcasted_iota(jnp.int32, (8, width), 0)
    halves = []
    for base in range(0, sources, 8):
        part = jnp.zeros((8, width), jnp.float32)
        for k in range(8):
            part = jnp.where(sub == k, moved_ref[base + k, data:data + 8, :].astype(jnp.float32), part)
        halves.append(part)
    halves.append(jnp.zeros((width - sources, width), jnp.float32))
    index = jnp.transpose(jnp.concatenate(halves, axis=0))
    for k in range(sources):
        spread[k * data:(k + 1) * data, :] = moved_ref[k, :data, :].astype(jnp.float32)
    total = sources * docs
    for block in range(2):
        where = []
        for slot in range(2):
            lane = block * 2 + slot
            where.append(jnp.concatenate(
                [jnp.broadcast_to(index[lane * docs:(lane + 1) * docs, k:k + 1], (docs, width))
                 for k in range(sources)], axis=0))
        first = spread[pl.ds(block * 2, total, stride=group), :]
        second = spread[pl.ds(block * 2 + 1, total, stride=group), :]
        first = jnp.where(where[0] == where[1], first + second, first)
        values[block * 2] = first.astype(jnp.bfloat16)
        values[block * 2 + 1] = second.astype(jnp.bfloat16)
        tiles[block * 2] = where[0].astype(jnp.bfloat16)
        tiles[block * 2 + 1] = where[1].astype(jnp.bfloat16)

    core = core_ref[0]
    tiles_step = depth // width

    out_ref[...] = jnp.zeros_like(out_ref)

    @pl.loop(0, 2 * STEPS)
    def _(step):
        pltpu.make_async_copy(own_ref.at[pl.ds(0, depth)], weights.at[step], sems.at[step]).wait()
        block = jnp.where(step < STEPS, core, 1 - core)
        base = (lax.rem(step, STEPS) * tiles_step).astype(jnp.float32)
        total = out_ref[...]
        for chunk in range(tiles_step // 2):
            parts = []
            for t in (2 * chunk, 2 * chunk + 1):
                mark = jnp.full((1, width), base + t, jnp.float32).astype(jnp.bfloat16)
                parts.append(jnp.where(
                    tiles[block * 2] == mark, values[block * 2],
                    jnp.where(tiles[block * 2 + 1] == mark, values[block * 2 + 1], jnp.zeros((), jnp.bfloat16))))
            dense = jnp.concatenate(parts, axis=1)
            total = total + jnp.dot(
                dense, weights[step, 2 * chunk * width:2 * (chunk + 1) * width, :],
                preferred_element_type=jnp.float32)
        out_ref[...] = total


def to_half(values, scale):
    return (values * scale).astype(jnp.float16)


def from_half(values, scale):
    return values.astype(jnp.float32) * (1.0 / scale)


def shards(counts, tile_index, tile_count, whitening, factors):
    doc_axes = ("zh", "x", "c")
    doc_devices = lax.axis_size(doc_axes)
    chips = doc_devices // 2
    doc_local = counts.shape[0]
    slots = counts.shape[1] // doc_devices
    width = counts.shape[2]
    topics = whitening.shape[1]
    half = doc_local * chips
    group = 2 * slots
    swap = [(0, 1), (1, 0)]
    vmem = pl.BlockSpec(memory_space=pltpu.VMEM)
    anywhere = pl.BlockSpec(memory_space=pl.ANY)

    side = lax.axis_index("zh").astype(jnp.int32)
    core = lax.axis_index("c").astype(jnp.int32)
    cross_axes = ("x", "c")
    targets = lax.axis_size(cross_axes)
    units = doc_local // 2 + 2
    packed = jax.ShapeDtypeStruct((targets, units, group, width), jnp.bfloat16)
    near, far = pl.pallas_call(
        pack_kernel,
        out_shape=(packed, packed),
        in_specs=[pl.BlockSpec(memory_space=pltpu.SMEM), vmem, vmem, anywhere],
        out_specs=(vmem, vmem),
        scratch_shapes=[pltpu.SemaphoreType.DMA((2 * targets,))],
        compiler_params=pltpu.CompilerParams(vmem_limit_bytes=61 << 20),
        cost_estimate=pl.CostEstimate(flops=1 << 20, bytes_accessed=2 << 20, transcendentals=0),
        name="pack",
    )(side.reshape(1), tile_index.T, tile_count.T, counts.reshape(doc_local, chips, group, width))
    far = lax.ppermute(far, "zh", swap)
    other = lax.ppermute(whitening, "c", swap)
    near = lax.all_to_all(near, cross_axes, 0, 0, tiled=True)

    gram_matrix = jnp.dot(factors.T, factors, precision=HIGH) / topics
    early = penalty * jnp.dot(factors, gram_matrix * gram_matrix, precision=HIGH)
    depth = whitening.shape[0] // STEPS
    quarter = half // 2

    def project(moved, after):
        return pl.pallas_call(
            project_kernel,
            out_shape=jax.ShapeDtypeStruct((quarter, topics), jnp.float32),
            in_specs=[pl.BlockSpec(memory_space=pltpu.SMEM), vmem, anywhere, anywhere, anywhere],
            out_specs=vmem,
            scratch_shapes=[
                pltpu.VMEM((2 * STEPS, depth, topics), jnp.bfloat16),
                pltpu.VMEM((quarter * group, width), jnp.float32),
                pltpu.VMEM((group, quarter, width), jnp.bfloat16),
                pltpu.VMEM((group, quarter, width), jnp.bfloat16),
                pltpu.SemaphoreType.DMA((2 * STEPS,)),
            ],
            compiler_params=pltpu.CompilerParams(vmem_limit_bytes=PROJECT_VMEM),
            cost_estimate=pl.CostEstimate(
                flops=4 * quarter * whitening.shape[0] * topics, bytes_accessed=10 << 20, transcendentals=0),
            name="project",
        )(core.reshape(1), moved.reshape(targets, units * group, width), whitening, other, after)

    near_terms = project(near, early)
    far, near_terms = lax.optimization_barrier((far, near_terms))
    far = lax.all_to_all(far, cross_axes, 0, 0, tiled=True)
    far_terms = project(far, near_terms)
    terms = jnp.concatenate([
        jnp.where(side == 0, near_terms, far_terms), jnp.where(side == 0, far_terms, near_terms)], axis=0)

    plane_axes = ("y", "x")
    plane = lax.axis_size(plane_axes)
    column = lax.axis_size("zl")
    part = half // plane
    sent = to_half(terms, term_scale).reshape(plane, part, topics)
    got = lax.all_to_all(sent, plane_axes, 0, 0, tiled=True)
    plane_sum = jnp.sum(got.astype(jnp.float32), axis=0) * (1.0 / term_scale)
    sent = jnp.broadcast_to(to_half(plane_sum, total_scale)[None], (column, part, topics))
    got = lax.all_to_all(sent, "zl", 0, 0, tiled=True)
    total = jnp.sum(got.astype(jnp.float32), axis=0) * (1.0 / total_scale)
    total = total + lax.ppermute(total, "zh", swap)
    sent = jnp.broadcast_to(to_half(total, total_scale)[None], (plane, part, topics))
    got = lax.all_to_all(sent, plane_axes, 0, 0, tiled=True)
    projected = from_half(got.reshape(half, topics), total_scale)

    scores = jnp.dot(projected, factors, precision=HIGH) * (1.0 / math.sqrt(topics))
    moment = jnp.dot(projected.T, scores * scores, precision=HIGH)
    return (moment + lax.ppermute(moment, "c", swap)) * (1.0 / (2 * half)) - early


def solution(mesh):
    fine = Mesh(mesh.devices.reshape(2, 4, 2, 4, 4), ("zh", "x", "c", "zl", "y"))
    doc, vocab = ("zh", "x", "c"), ("zl", "y")
    in_specs = (P(doc, vocab, None), P(doc, vocab), P(doc, vocab), P(doc + vocab, None), P())
    return jax.shard_map(shards, mesh=fine, in_specs=in_specs, out_specs=P(), check_vma=False)
```

```python
import math

import jax
import jax.numpy as jnp
from jax import lax
from jax.experimental import pallas as pl
from jax.experimental.pallas import tpu as pltpu
from jax.sharding import Mesh, PartitionSpec as P

penalty = 0.25
term_scale = 256.0
total_scale = 4.0
HIGH = lax.Precision.HIGH
STEPS = 4
AHEAD = 2


def pack_kernel(index_hbm, live_hbm, counts_ref, out_ref, index_ref, live_ref, packed, small_sems, in_sems, out_sems):
    targets, units, group, width = packed.shape
    chips = targets // 2
    docs = units - 2
    small = [
        pltpu.make_async_copy(index_hbm, index_ref, small_sems.at[0]),
        pltpu.make_async_copy(live_hbm, live_ref, small_sems.at[1]),
    ]
    for copy in small:
        copy.start()
    copies = []
    for target in range(targets):
        chip, core = target // 2, target % 2
        copy = pltpu.make_async_copy(
            counts_ref.at[pl.ds(core * docs, docs), chip], packed.at[target, pl.ds(0, docs)], in_sems.at[target])
        copy.start()
        copies.append(copy)
    for copy in small:
        copy.wait()
    slots = group // 2
    marked = []
    for lane in range(group):
        tile = index_ref[pl.ds(lane, chips, stride=group), :]
        live = live_ref[pl.ds(lane // slots, chips, stride=2), :]
        marked.append(jnp.where(lane % slots < live, tile, -1).astype(jnp.float32))
    for core in range(2):
        rows = jnp.concatenate([m[:, core * docs:(core + 1) * docs] for m in marked], axis=1)
        for chip in range(chips):
            row = jnp.broadcast_to(rows[chip:chip + 1, :], (2 * group, width))
            packed[chip * 2 + core, docs:docs + 2] = row.reshape(2, group, width).astype(packed.dtype)
    sends = []
    for target in range(targets):
        copies[target].wait()
        copy = pltpu.make_async_copy(packed.at[target], out_ref.at[target], out_sems.at[target])
        copy.start()
        sends.append(copy)
    for copy in sends:
        copy.wait()


def project_kernel(core_ref, moved_ref, own_ref, other_ref, early_ref, out_ref,
                   weights, spread, values, tiles, sems):
    sources, rows, width = moved_ref.shape
    group = 4
    data = rows - 2 * group
    docs = data // group
    depth = own_ref.shape[0] // STEPS

    def fetch(source, step):
        pltpu.make_async_copy(
            source.at[pl.ds(lax.rem(step, STEPS) * depth, depth)], weights.at[step], sems.at[step]).start()

    for step in range(AHEAD):
        fetch(own_ref, jnp.int32(step))

    sub = lax.broadcasted_iota(jnp.int32, (8, width), 0)
    halves = []
    for base in range(0, sources, 8):
        part = jnp.zeros((8, width), jnp.float32)
        for k in range(8):
            part = jnp.where(sub == k, moved_ref[base + k, data:data + 8, :].astype(jnp.float32), part)
        halves.append(part)
    halves.append(jnp.zeros((width - sources, width), jnp.float32))
    index = jnp.transpose(jnp.concatenate(halves, axis=0))
    for k in range(sources):
        spread[k * data:(k + 1) * data, :] = moved_ref[k, :data, :].astype(jnp.float32)
    total = sources * docs
    for block in range(2):
        where = []
        for slot in range(2):
            lane = block * 2 + slot
            where.append(jnp.concatenate(
                [jnp.broadcast_to(index[lane * docs:(lane + 1) * docs, k:k + 1], (docs, width))
                 for k in range(sources)], axis=0))
        first = spread[pl.ds(block * 2, total, stride=group), :]
        second = spread[pl.ds(block * 2 + 1, total, stride=group), :]
        first = jnp.where(where[0] == where[1], first + second, first)
        values[block * 2] = first.astype(jnp.bfloat16)
        values[block * 2 + 1] = second.astype(jnp.bfloat16)
        tiles[block * 2] = where[0].astype(jnp.bfloat16)
        tiles[block * 2 + 1] = where[1].astype(jnp.bfloat16)

    core = core_ref[0]
    tiles_step = depth // width

    out_ref[...] = jnp.zeros_like(out_ref)

    @pl.loop(0, 2 * STEPS)
    def _(step):
        pltpu.make_async_copy(own_ref.at[pl.ds(0, depth)], weights.at[step], sems.at[step]).wait()

        @pl.when(step + AHEAD < STEPS)
        def _():
            fetch(own_ref, step + AHEAD)

        @pl.when(jnp.logical_and(step + AHEAD >= STEPS, step + AHEAD < 2 * STEPS))
        def _():
            fetch(other_ref, step + AHEAD)

        block = jnp.where(step < STEPS, core, 1 - core)
        base = (lax.rem(step, STEPS) * tiles_step).astype(jnp.float32)
        total = out_ref[...]
        for chunk in range(tiles_step // 2):
            parts = []
            for t in (2 * chunk, 2 * chunk + 1):
                mark = jnp.full((1, width), base + t, jnp.float32).astype(jnp.bfloat16)
                parts.append(jnp.where(
                    tiles[block * 2] == mark, values[block * 2],
                    jnp.where(tiles[block * 2 + 1] == mark, values[block * 2 + 1], jnp.zeros((), jnp.bfloat16))))
            dense = jnp.concatenate(parts, axis=1)
            total = total + jnp.dot(
                dense, weights[step, 2 * chunk * width:2 * (chunk + 1) * width, :],
                preferred_element_type=jnp.float32)
        out_ref[...] = total


def to_half(values, scale):
    return (values * scale).astype(jnp.float16)


def from_half(values, scale):
    return values.astype(jnp.float32) * (1.0 / scale)


def shards(counts, tile_index, tile_count, whitening, factors):
    doc_axes = ("zh", "x", "c")
    doc_devices = lax.axis_size(doc_axes)
    chips = doc_devices // 2
    doc_local = counts.shape[0]
    slots = counts.shape[1] // doc_devices
    width = counts.shape[2]
    topics = whitening.shape[1]
    half = doc_local * chips
    group = 2 * slots
    swap = [(0, 1), (1, 0)]
    vmem = pl.BlockSpec(memory_space=pltpu.VMEM)
    anywhere = pl.BlockSpec(memory_space=pl.ANY)

    other = lax.ppermute(whitening, "c", swap)
    units = doc_local // 2 + 2
    packed = pl.pallas_call(
        pack_kernel,
        out_shape=jax.ShapeDtypeStruct((doc_devices, units, group, width), jnp.bfloat16),
        in_specs=[anywhere, anywhere, anywhere],
        out_specs=anywhere,
        scratch_shapes=[
            pltpu.VMEM(tile_index.shape[::-1], tile_index.dtype),
            pltpu.VMEM(tile_count.shape[::-1], tile_count.dtype),
            pltpu.VMEM((doc_devices, units, group, width), jnp.bfloat16),
            pltpu.SemaphoreType.DMA((2,)),
            pltpu.SemaphoreType.DMA((doc_devices,)),
            pltpu.SemaphoreType.DMA((doc_devices,)),
        ],
        compiler_params=pltpu.CompilerParams(vmem_limit_bytes=61 << 20),
        cost_estimate=pl.CostEstimate(flops=1 << 20, bytes_accessed=2 << 20, transcendentals=0),
        name="pack",
    )(tile_index.T, tile_count.T, counts.reshape(doc_local, chips, group, width))
    moved = lax.all_to_all(packed, doc_axes, 0, 0, tiled=True)
    moved = moved.reshape(doc_devices, units * group, width)

    gram_matrix = jnp.dot(factors.T, factors, precision=HIGH) / topics
    early = penalty * jnp.dot(factors, gram_matrix * gram_matrix, precision=HIGH)
    core = lax.axis_index("c")
    depth = whitening.shape[0] // STEPS
    terms = pl.pallas_call(
        project_kernel,
        out_shape=jax.ShapeDtypeStruct((half, topics), jnp.float32),
        in_specs=[pl.BlockSpec(memory_space=pltpu.SMEM), vmem, anywhere, anywhere, anywhere],
        out_specs=vmem,
        scratch_shapes=[
            pltpu.VMEM((2 * STEPS, depth, topics), jnp.bfloat16),
            pltpu.VMEM((half * group, width), jnp.float32),
            pltpu.VMEM((group, half, width), jnp.bfloat16),
            pltpu.VMEM((group, half, width), jnp.bfloat16),
            pltpu.SemaphoreType.DMA((2 * STEPS,)),
        ],
        compiler_params=pltpu.CompilerParams(vmem_limit_bytes=50 << 20),
        cost_estimate=pl.CostEstimate(
            flops=4 * half * whitening.shape[0] * topics, bytes_accessed=12 << 20, transcendentals=0),
        name="project",
    )(core.astype(jnp.int32).reshape(1), moved, whitening, other, early)

    plane_axes, column_axes = ("y", "x"), ("zh", "zl")
    plane = lax.axis_size(plane_axes)
    column = lax.axis_size(column_axes)
    part = half // plane
    sent = to_half(terms, term_scale).reshape(plane, part, topics)
    got = lax.all_to_all(sent, plane_axes, 0, 0, tiled=True)
    plane_sum = jnp.sum(got.astype(jnp.float32), axis=0) * (1.0 / term_scale)
    sent = jnp.broadcast_to(to_half(plane_sum, total_scale)[None], (column, part, topics))
    got = lax.all_to_all(sent, column_axes, 0, 0, tiled=True)
    total = jnp.sum(got.astype(jnp.float32), axis=0) * (1.0 / total_scale)
    sent = jnp.broadcast_to(to_half(total, total_scale)[None], (plane, part, topics))
    got = lax.all_to_all(sent, plane_axes, 0, 0, tiled=True)
    projected = from_half(got.reshape(half, topics), total_scale)

    scores = jnp.dot(projected, factors, precision=HIGH) * (1.0 / math.sqrt(topics))
    moment = jnp.dot(projected.T, scores * scores, precision=HIGH)
    return (moment + lax.ppermute(moment, "c", swap)) * (1.0 / (2 * half)) - early


def solution(mesh):
    fine = Mesh(mesh.devices.reshape(2, 4, 2, 4, 4), ("zh", "x", "c", "zl", "y"))
    doc, vocab = ("zh", "x", "c"), ("zl", "y")
    in_specs = (P(doc, vocab, None), P(doc, vocab), P(doc, vocab), P(doc + vocab, None), P())
    return jax.shard_map(shards, mesh=fine, in_specs=in_specs, out_specs=P(), check_vma=False)
```

```python
import functools
import math

import jax
import jax.numpy as jnp
from jax import lax
from jax.experimental import pallas as pl
from jax.experimental.pallas import tpu as pltpu
from jax.sharding import Mesh, PartitionSpec as P


penalty = 0.25
term_scale = 256.0
total_scale = 4.0
HIGH = lax.Precision.HIGH
STEPS = 4
AHEAD = 2


def pack_kernel(index_hbm, live_hbm, counts_ref, out_ref, index_ref, live_ref, packed, small_sems, in_sems, out_sems):
    targets, units, group, width = packed.shape
    chips = targets // 2
    docs = units - 2
    small = [
        pltpu.make_async_copy(index_hbm, index_ref, small_sems.at[0]),
        pltpu.make_async_copy(live_hbm, live_ref, small_sems.at[1]),
    ]
    for copy in small:
        copy.start()
    copies = []
    for target in range(targets):
        chip, core = target // 2, target % 2
        copy = pltpu.make_async_copy(
            counts_ref.at[pl.ds(core * docs, docs), chip], packed.at[target, pl.ds(0, docs)], in_sems.at[target])
        copy.start()
        copies.append(copy)
    for copy in small:
        copy.wait()
    slots = group // 2
    marked = []
    for lane in range(group):
        tile = index_ref[pl.ds(lane, chips, stride=group), :]
        live = live_ref[pl.ds(lane // slots, chips, stride=2), :]
        marked.append(jnp.where(lane % slots < live, tile, -1).astype(jnp.float32))
    for core in range(2):
        rows = jnp.concatenate([m[:, core * docs:(core + 1) * docs] for m in marked], axis=1)
        for chip in range(chips):
            row = jnp.broadcast_to(rows[chip:chip + 1, :], (2 * group, width))
            packed[chip * 2 + core, docs:docs + 2] = row.reshape(2, group, width).astype(packed.dtype)
    sends = []
    for target in range(targets):
        copies[target].wait()
        copy = pltpu.make_async_copy(packed.at[target], out_ref.at[target], out_sems.at[target])
        copy.start()
        sends.append(copy)
    for copy in sends:
        copy.wait()


def project_kernel(core_ref, moved_ref, own_ref, other_ref, early_ref, out_ref,
                   weights, spread, values, tiles, sems):
    sources, rows, width = moved_ref.shape
    group = 4
    data = rows - 2 * group
    docs = data // group
    depth = own_ref.shape[0] // STEPS

    def fetch(source, step):
        pltpu.make_async_copy(
            source.at[pl.ds(lax.rem(step, STEPS) * depth, depth)], weights.at[step], sems.at[step]).start()

    for step in range(AHEAD):
        fetch(own_ref, jnp.int32(step))

    sub = lax.broadcasted_iota(jnp.int32, (8, width), 0)
    halves = []
    for base in range(0, sources, 8):
        part = jnp.zeros((8, width), jnp.float32)
        for k in range(8):
            part = jnp.where(sub == k, moved_ref[base + k, data:data + 8, :].astype(jnp.float32), part)
        halves.append(part)
    halves.append(jnp.zeros((width - sources, width), jnp.float32))
    index = jnp.transpose(jnp.concatenate(halves, axis=0))
    for k in range(sources):
        spread[k * data:(k + 1) * data, :] = moved_ref[k, :data, :].astype(jnp.float32)
    total = sources * docs
    for block in range(2):
        where = []
        for slot in range(2):
            lane = block * 2 + slot
            where.append(jnp.concatenate(
                [jnp.broadcast_to(index[lane * docs:(lane + 1) * docs, k:k + 1], (docs, width))
                 for k in range(sources)], axis=0))
        first = spread[pl.ds(block * 2, total, stride=group), :]
        second = spread[pl.ds(block * 2 + 1, total, stride=group), :]
        first = jnp.where(where[0] == where[1], first + second, first)
        values[block * 2] = first.astype(jnp.bfloat16)
        values[block * 2 + 1] = second.astype(jnp.bfloat16)
        tiles[block * 2] = where[0].astype(jnp.bfloat16)
        tiles[block * 2 + 1] = where[1].astype(jnp.bfloat16)

    core = core_ref[0]
    tiles_step = depth // width

    out_ref[...] = jnp.zeros_like(out_ref)

    @pl.loop(0, 2 * STEPS)
    def _(step):
        pltpu.make_async_copy(own_ref.at[pl.ds(0, depth)], weights.at[step], sems.at[step]).wait()

        @pl.when(step + AHEAD < STEPS)
        def _():
            fetch(own_ref, step + AHEAD)

        @pl.when(jnp.logical_and(step + AHEAD >= STEPS, step + AHEAD < 2 * STEPS))
        def _():
            fetch(other_ref, step + AHEAD)

        block = jnp.where(step < STEPS, core, 1 - core)
        base = (lax.rem(step, STEPS) * tiles_step).astype(jnp.float32)
        total = out_ref[...]
        for chunk in range(tiles_step // 2):
            parts = []
            for t in (2 * chunk, 2 * chunk + 1):
                mark = jnp.full((1, width), base + t, jnp.float32).astype(jnp.bfloat16)
                parts.append(jnp.where(
                    tiles[block * 2] == mark, values[block * 2],
                    jnp.where(tiles[block * 2 + 1] == mark, values[block * 2 + 1], jnp.zeros((), jnp.bfloat16))))
            dense = jnp.concatenate(parts, axis=1)
            total = total + jnp.dot(
                dense, weights[step, 2 * chunk * width:2 * (chunk + 1) * width, :],
                preferred_element_type=jnp.float32)
        out_ref[...] = total


def combine_kernel(scale, made_a, got_a, made_b, got_b, early_ref, out_ref):
    share = made_a.shape[0]
    out_ref[:share, :] = (made_a[...] + got_a[...]) * scale - early_ref[:share, :]
    out_ref[share:, :] = (made_b[...] + got_b[...]) * scale - early_ref[share:, :]


def to_half(values, scale):
    return (values * scale).astype(jnp.float16)


def from_half(values, scale):
    return values.astype(jnp.float32) * (1.0 / scale)


def shards(counts, tile_index, tile_count, whitening, factors):
    doc_axes = ("zh", "x", "c")
    doc_devices = lax.axis_size(doc_axes)
    chips = doc_devices // 2
    doc_local = counts.shape[0]
    slots = counts.shape[1] // doc_devices
    width = counts.shape[2]
    topics = whitening.shape[1]
    half = doc_local * chips
    group = 2 * slots
    swap = [(0, 1), (1, 0)]
    vmem = pl.BlockSpec(memory_space=pltpu.VMEM)
    anywhere = pl.BlockSpec(memory_space=pl.ANY)

    other = lax.ppermute(whitening, "c", swap)
    units = doc_local // 2 + 2
    packed = pl.pallas_call(
        pack_kernel,
        out_shape=jax.ShapeDtypeStruct((doc_devices, units, group, width), jnp.bfloat16),
        in_specs=[anywhere, anywhere, anywhere],
        out_specs=anywhere,
        scratch_shapes=[
            pltpu.VMEM(tile_index.shape[::-1], tile_index.dtype),
            pltpu.VMEM(tile_count.shape[::-1], tile_count.dtype),
            pltpu.VMEM((doc_devices, units, group, width), jnp.bfloat16),
            pltpu.SemaphoreType.DMA((2,)),
            pltpu.SemaphoreType.DMA((doc_devices,)),
            pltpu.SemaphoreType.DMA((doc_devices,)),
        ],
        compiler_params=pltpu.CompilerParams(vmem_limit_bytes=61 << 20),
        cost_estimate=pl.CostEstimate(flops=1 << 20, bytes_accessed=2 << 20, transcendentals=0),
        name="pack",
    )(tile_index.T, tile_count.T, counts.reshape(doc_local, chips, group, width))
    moved = lax.all_to_all(packed, doc_axes, 0, 0, tiled=True)
    moved = moved.reshape(doc_devices, units * group, width)

    gram_matrix = jnp.dot(factors.T, factors, precision=HIGH) / topics
    early = penalty * jnp.dot(factors, gram_matrix * gram_matrix, precision=HIGH)
    core = lax.axis_index("c")
    depth = whitening.shape[0] // STEPS
    terms = pl.pallas_call(
        project_kernel,
        out_shape=jax.ShapeDtypeStruct((half, topics), jnp.float32),
        in_specs=[pl.BlockSpec(memory_space=pltpu.SMEM), vmem, anywhere, anywhere, anywhere],
        out_specs=vmem,
        scratch_shapes=[
            pltpu.VMEM((2 * STEPS, depth, topics), jnp.bfloat16),
            pltpu.VMEM((half * group, width), jnp.float32),
            pltpu.VMEM((group, half, width), jnp.bfloat16),
            pltpu.VMEM((group, half, width), jnp.bfloat16),
            pltpu.SemaphoreType.DMA((2 * STEPS,)),
        ],
        compiler_params=pltpu.CompilerParams(vmem_limit_bytes=50 << 20),
        cost_estimate=pl.CostEstimate(
            flops=4 * half * whitening.shape[0] * topics, bytes_accessed=12 << 20, transcendentals=0),
        name="project",
    )(core.astype(jnp.int32).reshape(1), moved, whitening, other, early)

    plane_axes, column_axes = ("y", "x"), ("zl", "zh")
    plane = lax.axis_size(plane_axes)
    column = lax.axis_size(column_axes)
    part = half // plane
    sent = to_half(terms, term_scale).reshape(plane, part, topics)
    got = lax.all_to_all(sent, plane_axes, 0, 0, tiled=True)
    plane_sum = jnp.sum(got.astype(jnp.float32), axis=0) * (1.0 / term_scale)
    sent = jnp.broadcast_to(to_half(plane_sum, total_scale)[None], (column, part, topics))
    got = lax.all_to_all(sent, column_axes, 0, 0, tiled=True)
    total = jnp.sum(got.astype(jnp.float32), axis=0) * (1.0 / total_scale)
    sent = jnp.broadcast_to(to_half(total, total_scale)[None], (plane, part, topics))
    got = lax.all_to_all(sent, plane_axes, 0, 0, tiled=True)
    projected = from_half(got.reshape(half, topics), total_scale)

    scores = jnp.dot(projected, factors, precision=HIGH) * (1.0 / math.sqrt(topics))
    squares = scores * scores
    share = topics // 2
    made, got = [], []
    for k in range(2):
        made.append(jnp.dot(projected[:, k * share:(k + 1) * share].T, squares, precision=HIGH))
        got.append(lax.ppermute(made[k], "c", swap))
    return pl.pallas_call(
        functools.partial(combine_kernel, 1.0 / (2 * half)),
        out_shape=jax.ShapeDtypeStruct((topics, topics), jnp.float32),
        in_specs=[vmem] * 5,
        out_specs=vmem,
        compiler_params=pltpu.CompilerParams(vmem_limit_bytes=16 << 20),
        name="combine",
    )(made[0], got[0], made[1], got[1], early)


def solution(mesh):
    fine = Mesh(mesh.devices.reshape(2, 4, 2, 4, 4), ("zh", "x", "c", "zl", "y"))
    doc, vocab = ("zh", "x", "c"), ("zl", "y")
    in_specs = (P(doc, vocab, None), P(doc, vocab), P(doc, vocab), P(doc + vocab, None), P())
    return jax.shard_map(shards, mesh=fine, in_specs=in_specs, out_specs=P(), check_vma=False)
```

```python
import functools
import math

import jax
import jax.numpy as jnp
from jax import lax
from jax.experimental import pallas as pl
from jax.experimental.pallas import tpu as pltpu
from jax.sharding import Mesh, PartitionSpec as P


penalty = 0.25
term_scale = 256.0
total_scale = 4.0
HIGH = lax.Precision.HIGH
STEPS = 4
AHEAD = 2


def pack_kernel(index_hbm, live_hbm, counts_ref, out_ref, index_ref, live_ref, packed, small_sems, in_sems, out_sems):
    targets, units, group, width = packed.shape
    chips = targets // 2
    docs = units - 2
    small = [
        pltpu.make_async_copy(index_hbm, index_ref, small_sems.at[0]),
        pltpu.make_async_copy(live_hbm, live_ref, small_sems.at[1]),
    ]
    for copy in small:
        copy.start()
    copies = []
    for target in range(targets):
        chip, core = target // 2, target % 2
        place = core * chips + (chip % (chips // 2)) * 2 + chip // (chips // 2)
        copy = pltpu.make_async_copy(
            counts_ref.at[pl.ds(core * docs, docs), chip], packed.at[place, pl.ds(0, docs)], in_sems.at[target])
        copy.start()
        copies.append(copy)
    for copy in small:
        copy.wait()
    slots = group // 2
    marked = []
    for lane in range(group):
        tile = index_ref[pl.ds(lane, chips, stride=group), :]
        live = live_ref[pl.ds(lane // slots, chips, stride=2), :]
        marked.append(jnp.where(lane % slots < live, tile, -1).astype(jnp.float32))
    for core in range(2):
        rows = jnp.concatenate([m[:, core * docs:(core + 1) * docs] for m in marked], axis=1)
        for chip in range(chips):
            row = jnp.broadcast_to(rows[chip:chip + 1, :], (2 * group, width))
            packed[core * chips + (chip % (chips // 2)) * 2 + chip // (chips // 2), docs:docs + 2] = row.reshape(2, group, width).astype(packed.dtype)
    sends = []
    for copy in copies:
        copy.wait()
    for target in range(targets):
        copy = pltpu.make_async_copy(packed.at[target], out_ref.at[target], out_sems.at[target])
        copy.start()
        sends.append(copy)
    for copy in sends:
        copy.wait()


def project_kernel(core_ref, moved_ref, own_ref, other_ref, early_ref, out_ref,
                   weights, spread, values, tiles, sems):
    sources, rows, width = moved_ref.shape
    group = 4
    data = rows - 2 * group
    docs = data // group
    depth = own_ref.shape[0] // STEPS

    def fetch(source, step):
        pltpu.make_async_copy(
            source.at[pl.ds(lax.rem(step, STEPS) * depth, depth)], weights.at[step], sems.at[step]).start()

    for step in range(AHEAD):
        fetch(own_ref, jnp.int32(step))

    sub = lax.broadcasted_iota(jnp.int32, (8, width), 0)
    halves = []
    for base in range(0, sources, 8):
        part = jnp.zeros((8, width), jnp.float32)
        for k in range(8):
            part = jnp.where(sub == k, moved_ref[base + k, data:data + 8, :].astype(jnp.float32), part)
        halves.append(part)
    halves.append(jnp.zeros((width - sources, width), jnp.float32))
    index = jnp.transpose(jnp.concatenate(halves, axis=0))
    for k in range(sources):
        spread[k * data:(k + 1) * data, :] = moved_ref[k, :data, :].astype(jnp.float32)
    total = sources * docs
    for block in range(2):
        where = []
        for slot in range(2):
            lane = block * 2 + slot
            where.append(jnp.concatenate(
                [jnp.broadcast_to(index[lane * docs:(lane + 1) * docs, k:k + 1], (docs, width))
                 for k in range(sources)], axis=0))
        first = spread[pl.ds(block * 2, total, stride=group), :]
        second = spread[pl.ds(block * 2 + 1, total, stride=group), :]
        first = jnp.where(where[0] == where[1], first + second, first)
        values[block * 2] = first.astype(jnp.bfloat16)
        values[block * 2 + 1] = second.astype(jnp.bfloat16)
        tiles[block * 2] = where[0].astype(jnp.bfloat16)
        tiles[block * 2 + 1] = where[1].astype(jnp.bfloat16)

    core = core_ref[0]
    tiles_step = depth // width

    out_ref[...] = jnp.zeros_like(out_ref)

    @pl.loop(0, 2 * STEPS)
    def _(step):
        pltpu.make_async_copy(own_ref.at[pl.ds(0, depth)], weights.at[step], sems.at[step]).wait()

        @pl.when(step + AHEAD < STEPS)
        def _():
            fetch(own_ref, step + AHEAD)

        @pl.when(jnp.logical_and(step + AHEAD >= STEPS, step + AHEAD < 2 * STEPS))
        def _():
            fetch(other_ref, step + AHEAD)

        block = jnp.where(step < STEPS, core, 1 - core)
        base = (lax.rem(step, STEPS) * tiles_step).astype(jnp.float32)
        total = out_ref[...]
        for chunk in range(tiles_step // 2):
            parts = []
            for t in (2 * chunk, 2 * chunk + 1):
                mark = jnp.full((1, width), base + t, jnp.float32).astype(jnp.bfloat16)
                parts.append(jnp.where(
                    tiles[block * 2] == mark, values[block * 2],
                    jnp.where(tiles[block * 2 + 1] == mark, values[block * 2 + 1], jnp.zeros((), jnp.bfloat16))))
            dense = jnp.concatenate(parts, axis=1)
            total = total + jnp.dot(
                dense, weights[step, 2 * chunk * width:2 * (chunk + 1) * width, :],
                preferred_element_type=jnp.float32)
        out_ref[...] = total


def combine_kernel(scale, made_a, got_a, made_b, got_b, early_ref, out_ref):
    share = made_a.shape[0]
    out_ref[:share, :] = (made_a[...] + got_a[...]) * scale - early_ref[:share, :]
    out_ref[share:, :] = (made_b[...] + got_b[...]) * scale - early_ref[share:, :]


def to_half(values, scale):
    return (values * scale).astype(jnp.float16)


def from_half(values, scale):
    return values.astype(jnp.float32) * (1.0 / scale)


def shards(counts, tile_index, tile_count, whitening, factors):
    doc_axes = ('c', 'x', 'zh')
    doc_devices = lax.axis_size(doc_axes)
    chips = doc_devices // 2
    doc_local = counts.shape[0]
    slots = counts.shape[1] // doc_devices
    width = counts.shape[2]
    topics = whitening.shape[1]
    half = doc_local * chips
    group = 2 * slots
    swap = [(0, 1), (1, 0)]
    vmem = pl.BlockSpec(memory_space=pltpu.VMEM)
    anywhere = pl.BlockSpec(memory_space=pl.ANY)

    other = lax.ppermute(whitening, "c", swap)
    units = doc_local // 2 + 2
    packed = pl.pallas_call(
        pack_kernel,
        out_shape=jax.ShapeDtypeStruct((doc_devices, units, group, width), jnp.bfloat16),
        in_specs=[anywhere, anywhere, anywhere],
        out_specs=anywhere,
        scratch_shapes=[
            pltpu.VMEM(tile_index.shape[::-1], tile_index.dtype),
            pltpu.VMEM(tile_count.shape[::-1], tile_count.dtype),
            pltpu.VMEM((doc_devices, units, group, width), jnp.bfloat16),
            pltpu.SemaphoreType.DMA((2,)),
            pltpu.SemaphoreType.DMA((doc_devices,)),
            pltpu.SemaphoreType.DMA((doc_devices,)),
        ],
        compiler_params=pltpu.CompilerParams(vmem_limit_bytes=61 << 20),
        cost_estimate=pl.CostEstimate(flops=1 << 20, bytes_accessed=2 << 20, transcendentals=0),
        name="pack",
    )(tile_index.T, tile_count.T, counts.reshape(doc_local, chips, group, width))
    moved = lax.all_to_all(packed, doc_axes, 0, 0, tiled=True)
    moved = moved.reshape(doc_devices, units * group, width)

    gram_matrix = jnp.dot(factors.T, factors, precision=HIGH) / topics
    early = penalty * jnp.dot(factors, gram_matrix * gram_matrix, precision=HIGH)
    core = lax.axis_index("c")
    depth = whitening.shape[0] // STEPS
    terms = pl.pallas_call(
        project_kernel,
        out_shape=jax.ShapeDtypeStruct((half, topics), jnp.float32),
        in_specs=[pl.BlockSpec(memory_space=pltpu.SMEM), vmem, anywhere, anywhere, anywhere],
        out_specs=vmem,
        scratch_shapes=[
            pltpu.VMEM((2 * STEPS, depth, topics), jnp.bfloat16),
            pltpu.VMEM((half * group, width), jnp.float32),
            pltpu.VMEM((group, half, width), jnp.bfloat16),
            pltpu.VMEM((group, half, width), jnp.bfloat16),
            pltpu.SemaphoreType.DMA((2 * STEPS,)),
        ],
        compiler_params=pltpu.CompilerParams(vmem_limit_bytes=50 << 20),
        cost_estimate=pl.CostEstimate(
            flops=4 * half * whitening.shape[0] * topics, bytes_accessed=12 << 20, transcendentals=0),
        name="project",
    )(core.astype(jnp.int32).reshape(1), moved, whitening, other, early)

    plane_axes, column_axes = ("y", "x"), ("zl", "zh")
    plane = lax.axis_size(plane_axes)
    column = lax.axis_size(column_axes)
    part = half // plane
    sent = to_half(terms, term_scale).reshape(plane, part, topics)
    got = lax.all_to_all(sent, plane_axes, 0, 0, tiled=True)
    plane_sum = jnp.sum(got.astype(jnp.float32), axis=0) * (1.0 / term_scale)
    sent = jnp.broadcast_to(to_half(plane_sum, total_scale)[None], (column, part, topics))
    got = lax.all_to_all(sent, column_axes, 0, 0, tiled=True)
    total = jnp.sum(got.astype(jnp.float32), axis=0) * (1.0 / total_scale)
    sent = jnp.broadcast_to(to_half(total, total_scale)[None], (plane, part, topics))
    got = lax.all_to_all(sent, plane_axes, 0, 0, tiled=True)
    projected = from_half(got.reshape(half, topics), total_scale)

    scores = jnp.dot(projected, factors, precision=HIGH) * (1.0 / math.sqrt(topics))
    squares = scores * scores
    share = topics // 2
    made, got = [], []
    for k in range(2):
        made.append(jnp.dot(projected[:, k * share:(k + 1) * share].T, squares, precision=HIGH))
        got.append(lax.ppermute(made[k], "c", swap))
    return pl.pallas_call(
        functools.partial(combine_kernel, 1.0 / (2 * half)),
        out_shape=jax.ShapeDtypeStruct((topics, topics), jnp.float32),
        in_specs=[vmem] * 5,
        out_specs=vmem,
        compiler_params=pltpu.CompilerParams(vmem_limit_bytes=16 << 20),
        name="combine",
    )(made[0], got[0], made[1], got[1], early)


def solution(mesh):
    fine = Mesh(mesh.devices.reshape(2, 4, 2, 4, 4), ("zh", "x", "c", "zl", "y"))
    doc, vocab = ("zh", "x", "c"), ("zl", "y")
    in_specs = (P(doc, vocab, None), P(doc, vocab), P(doc, vocab), P(doc + vocab, None), P())
    return jax.shard_map(shards, mesh=fine, in_specs=in_specs, out_specs=P(), check_vma=False)
```

```python
import functools
import math

import jax
import jax.numpy as jnp
from jax import lax
from jax.experimental import pallas as pl
from jax.experimental.pallas import tpu as pltpu
from jax.sharding import Mesh, PartitionSpec as P


penalty = 0.25
term_scale = 256.0
total_scale = 4.0
HIGH = lax.Precision.HIGH
STEPS = 2
AHEAD = 2


def pack_kernel(index_hbm, live_hbm, counts_ref, out_ref, index_ref, live_ref, packed, small_sems, in_sems, out_sems):
    targets, units, group, width = packed.shape
    chips = targets // 2
    docs = units - 2
    small = [
        pltpu.make_async_copy(index_hbm, index_ref, small_sems.at[0]),
        pltpu.make_async_copy(live_hbm, live_ref, small_sems.at[1]),
    ]
    for copy in small:
        copy.start()
    copies = []
    for target in range(targets):
        chip, core = target // 2, target % 2
        place = core * chips + (chip % (chips // 2)) * 2 + chip // (chips // 2)
        copy = pltpu.make_async_copy(
            counts_ref.at[pl.ds(core * docs, docs), chip], packed.at[place, pl.ds(0, docs)], in_sems.at[place])
        copy.start()
        copies.append((place, copy))
    for copy in small:
        copy.wait()
    slots = group // 2
    marked = []
    for lane in range(group):
        tile = index_ref[pl.ds(lane, chips, stride=group), :]
        live = live_ref[pl.ds(lane // slots, chips, stride=2), :]
        marked.append(jnp.where(lane % slots < live, tile, -1).astype(jnp.float32))
    for core in range(2):
        rows = jnp.concatenate([m[:, core * docs:(core + 1) * docs] for m in marked], axis=1)
        for chip in range(chips):
            row = jnp.broadcast_to(rows[chip:chip + 1, :], (2 * group, width))
            packed[core * chips + (chip % (chips // 2)) * 2 + chip // (chips // 2), docs:docs + 2] = row.reshape(2, group, width).astype(packed.dtype)
    sends = []
    for place, copy in copies:
        copy.wait()
        copy = pltpu.make_async_copy(packed.at[place], out_ref.at[place], out_sems.at[place])
        copy.start()
        sends.append(copy)
    for copy in sends:
        copy.wait()


def project_kernel(core_ref, moved_ref, own_ref, other_ref, early_ref, out_ref,
                   weights, spread, values, tiles, sems):
    sources, rows, width = moved_ref.shape
    group = 4
    data = rows - 2 * group
    docs = data // group
    depth = own_ref.shape[0] // STEPS

    def fetch(source, step):
        pltpu.make_async_copy(
            source.at[pl.ds(lax.rem(step, STEPS) * depth, depth)], weights.at[step], sems.at[step]).start()

    for step in range(AHEAD):
        fetch(own_ref, jnp.int32(step))

    sub = lax.broadcasted_iota(jnp.int32, (8, width), 0)
    halves = []
    for base in range(0, sources, 8):
        part = jnp.zeros((8, width), jnp.float32)
        for k in range(8):
            part = jnp.where(sub == k, moved_ref[base + k, data:data + 8, :].astype(jnp.float32), part)
        halves.append(part)
    halves.append(jnp.zeros((width - sources, width), jnp.float32))
    index = jnp.transpose(jnp.concatenate(halves, axis=0))
    for k in range(sources):
        spread[k * data:(k + 1) * data, :] = moved_ref[k, :data, :].astype(jnp.float32)
    total = sources * docs
    for block in range(2):
        where = []
        for slot in range(2):
            lane = block * 2 + slot
            where.append(jnp.concatenate(
                [jnp.broadcast_to(index[lane * docs:(lane + 1) * docs, k:k + 1], (docs, width))
                 for k in range(sources)], axis=0))
        first = spread[pl.ds(block * 2, total, stride=group), :]
        second = spread[pl.ds(block * 2 + 1, total, stride=group), :]
        first = jnp.where(where[0] == where[1], first + second, first)
        values[block * 2] = first.astype(jnp.bfloat16)
        values[block * 2 + 1] = second.astype(jnp.bfloat16)
        tiles[block * 2] = where[0].astype(jnp.bfloat16)
        tiles[block * 2 + 1] = where[1].astype(jnp.bfloat16)

    core = core_ref[0]
    tiles_step = depth // width

    out_ref[...] = jnp.zeros_like(out_ref)

    @pl.loop(0, 2 * STEPS)
    def _(step):
        pltpu.make_async_copy(own_ref.at[pl.ds(0, depth)], weights.at[step], sems.at[step]).wait()

        @pl.when(step + AHEAD < STEPS)
        def _():
            fetch(own_ref, step + AHEAD)

        @pl.when(jnp.logical_and(step + AHEAD >= STEPS, step + AHEAD < 2 * STEPS))
        def _():
            fetch(other_ref, step + AHEAD)

        block = jnp.where(step < STEPS, core, 1 - core)
        base = (lax.rem(step, STEPS) * tiles_step).astype(jnp.float32)
        total = out_ref[...]
        for chunk in range(tiles_step // 2):
            parts = []
            for t in (2 * chunk, 2 * chunk + 1):
                mark = jnp.full((1, width), base + t, jnp.float32).astype(jnp.bfloat16)
                parts.append(jnp.where(
                    tiles[block * 2] == mark, values[block * 2],
                    jnp.where(tiles[block * 2 + 1] == mark, values[block * 2 + 1], jnp.zeros((), jnp.bfloat16))))
            dense = jnp.concatenate(parts, axis=1)
            total = total + jnp.dot(
                dense, weights[step, 2 * chunk * width:2 * (chunk + 1) * width, :],
                preferred_element_type=jnp.float32)
        out_ref[...] = total


def combine_kernel(scale, made_a, got_a, made_b, got_b, early_ref, out_ref):
    share = made_a.shape[0]
    out_ref[:share, :] = (made_a[...] + got_a[...]) * scale - early_ref[:share, :]
    out_ref[share:, :] = (made_b[...] + got_b[...]) * scale - early_ref[share:, :]


def to_half(values, scale):
    return (values * scale).astype(jnp.float16)


def from_half(values, scale):
    return values.astype(jnp.float32) * (1.0 / scale)


def shards(counts, tile_index, tile_count, whitening, factors):
    doc_axes = ('c', 'x', 'zh')
    doc_devices = lax.axis_size(doc_axes)
    chips = doc_devices // 2
    doc_local = counts.shape[0]
    slots = counts.shape[1] // doc_devices
    width = counts.shape[2]
    topics = whitening.shape[1]
    half = doc_local * chips
    group = 2 * slots
    swap = [(0, 1), (1, 0)]
    vmem = pl.BlockSpec(memory_space=pltpu.VMEM)
    anywhere = pl.BlockSpec(memory_space=pl.ANY)

    other = lax.ppermute(whitening, "c", swap)
    units = doc_local // 2 + 2
    packed = pl.pallas_call(
        pack_kernel,
        out_shape=jax.ShapeDtypeStruct((doc_devices, units, group, width), jnp.bfloat16),
        in_specs=[anywhere, anywhere, anywhere],
        out_specs=anywhere,
        scratch_shapes=[
            pltpu.VMEM(tile_index.shape[::-1], tile_index.dtype),
            pltpu.VMEM(tile_count.shape[::-1], tile_count.dtype),
            pltpu.VMEM((doc_devices, units, group, width), jnp.bfloat16),
            pltpu.SemaphoreType.DMA((2,)),
            pltpu.SemaphoreType.DMA((doc_devices,)),
            pltpu.SemaphoreType.DMA((doc_devices,)),
        ],
        compiler_params=pltpu.CompilerParams(vmem_limit_bytes=61 << 20),
        cost_estimate=pl.CostEstimate(flops=1 << 20, bytes_accessed=2 << 20, transcendentals=0),
        name="pack",
    )(tile_index.T, tile_count.T, counts.reshape(doc_local, chips, group, width))
    moved = lax.all_to_all(packed, doc_axes, 0, 0, tiled=True)
    moved = moved.reshape(doc_devices, units * group, width)

    gram_matrix = jnp.dot(factors.T, factors, precision=HIGH) / topics
    early = penalty * jnp.dot(factors, gram_matrix * gram_matrix, precision=HIGH)
    core = lax.axis_index("c")
    depth = whitening.shape[0] // STEPS
    terms = pl.pallas_call(
        project_kernel,
        out_shape=jax.ShapeDtypeStruct((half, topics), jnp.float32),
        in_specs=[pl.BlockSpec(memory_space=pltpu.SMEM), vmem, anywhere, anywhere, anywhere],
        out_specs=vmem,
        scratch_shapes=[
            pltpu.VMEM((2 * STEPS, depth, topics), jnp.bfloat16),
            pltpu.VMEM((half * group, width), jnp.float32),
            pltpu.VMEM((group, half, width), jnp.bfloat16),
            pltpu.VMEM((group, half, width), jnp.bfloat16),
            pltpu.SemaphoreType.DMA((2 * STEPS,)),
        ],
        compiler_params=pltpu.CompilerParams(vmem_limit_bytes=50 << 20),
        cost_estimate=pl.CostEstimate(
            flops=4 * half * whitening.shape[0] * topics, bytes_accessed=12 << 20, transcendentals=0),
        name="project",
    )(core.astype(jnp.int32).reshape(1), moved, whitening, other, early)

    plane_axes, column_axes = ("y", "x"), ("zl", "zh")
    plane = lax.axis_size(plane_axes)
    column = lax.axis_size(column_axes)
    part = half // plane
    sent = to_half(terms, term_scale).reshape(plane, part, topics)
    got = lax.all_to_all(sent, plane_axes, 0, 0, tiled=True)
    plane_sum = jnp.sum(got.astype(jnp.float32), axis=0) * (1.0 / term_scale)
    sent = jnp.broadcast_to(to_half(plane_sum, total_scale)[None], (column, part, topics))
    got = lax.all_to_all(sent, column_axes, 0, 0, tiled=True)
    total = jnp.sum(got.astype(jnp.float32), axis=0) * (1.0 / total_scale)
    sent = jnp.broadcast_to(to_half(total, total_scale)[None], (plane, part, topics))
    got = lax.all_to_all(sent, plane_axes, 0, 0, tiled=True)
    projected = from_half(got.reshape(half, topics), total_scale)

    scores = jnp.dot(projected, factors, precision=HIGH) * (1.0 / math.sqrt(topics))
    squares = scores * scores
    share = topics // 2
    made, got = [], []
    for k in range(2):
        made.append(jnp.dot(projected[:, k * share:(k + 1) * share].T, squares, precision=HIGH))
        got.append(lax.ppermute(made[k], "c", swap))
    return pl.pallas_call(
        functools.partial(combine_kernel, 1.0 / (2 * half)),
        out_shape=jax.ShapeDtypeStruct((topics, topics), jnp.float32),
        in_specs=[vmem] * 5,
        out_specs=vmem,
        compiler_params=pltpu.CompilerParams(vmem_limit_bytes=16 << 20),
        name="combine",
    )(made[0], got[0], made[1], got[1], early)


def solution(mesh):
    fine = Mesh(mesh.devices.reshape(2, 4, 2, 4, 4), ("zh", "x", "c", "zl", "y"))
    doc, vocab = ("zh", "x", "c"), ("zl", "y")
    in_specs = (P(doc, vocab, None), P(doc, vocab), P(doc, vocab), P(doc + vocab, None), P())
    return jax.shard_map(shards, mesh=fine, in_specs=in_specs, out_specs=P(), check_vma=False)
```

```python
import functools
import math

import jax
import jax.numpy as jnp
from jax import lax
from jax.experimental import pallas as pl
from jax.experimental.pallas import tpu as pltpu
from jax.sharding import Mesh, PartitionSpec as P


penalty = 0.25
term_scale = 256.0
total_scale = 4.0
HIGH = lax.Precision.HIGH
STEPS = 1
AHEAD = 2


def pack_kernel(index_hbm, live_hbm, counts_ref, out_ref, index_ref, live_ref, packed, small_sems, in_sems, out_sems):
    targets, units, group, width = packed.shape
    chips = targets // 2
    docs = units - 2
    small = [
        pltpu.make_async_copy(index_hbm, index_ref, small_sems.at[0]),
        pltpu.make_async_copy(live_hbm, live_ref, small_sems.at[1]),
    ]
    for copy in small:
        copy.start()
    copies = []
    for target in range(targets):
        chip, core = target // 2, target % 2
        place = core * chips + (chip % (chips // 2)) * 2 + chip // (chips // 2)
        copy = pltpu.make_async_copy(
            counts_ref.at[pl.ds(core * docs, docs), chip], packed.at[place, pl.ds(0, docs)], in_sems.at[place])
        copy.start()
        copies.append((place, copy))
    for copy in small:
        copy.wait()
    slots = group // 2
    marked = []
    for lane in range(group):
        tile = index_ref[pl.ds(lane, chips, stride=group), :]
        live = live_ref[pl.ds(lane // slots, chips, stride=2), :]
        marked.append(jnp.where(lane % slots < live, tile, -1).astype(jnp.float32))
    for core in range(2):
        rows = jnp.concatenate([m[:, core * docs:(core + 1) * docs] for m in marked], axis=1)
        for chip in range(chips):
            row = jnp.broadcast_to(rows[chip:chip + 1, :], (2 * group, width))
            packed[core * chips + (chip % (chips // 2)) * 2 + chip // (chips // 2), docs:docs + 2] = row.reshape(2, group, width).astype(packed.dtype)
    sends = []
    for place, copy in copies:
        copy.wait()
        copy = pltpu.make_async_copy(packed.at[place], out_ref.at[place], out_sems.at[place])
        copy.start()
        sends.append(copy)
    for copy in sends:
        copy.wait()


def project_kernel(core_ref, moved_ref, own_ref, other_ref, early_ref, out_ref,
                   weights, spread, values, tiles, sems):
    sources, rows, width = moved_ref.shape
    group = 4
    data = rows - 2 * group
    docs = data // group
    depth = own_ref.shape[0] // STEPS
    unit = depth // 2
    units = 4 * STEPS

    def fetch(source, k):
        pltpu.make_async_copy(
            source.at[pl.ds(lax.rem(k, units // 2) * unit, unit)], weights.at[k], sems.at[k]).start()

    for k in range(AHEAD):
        fetch(own_ref, jnp.int32(k))

    sub = lax.broadcasted_iota(jnp.int32, (8, width), 0)
    halves = []
    for base in range(0, sources, 8):
        part = jnp.zeros((8, width), jnp.float32)
        for k in range(8):
            part = jnp.where(sub == k, moved_ref[base + k, data:data + 8, :].astype(jnp.float32), part)
        halves.append(part)
    halves.append(jnp.zeros((width - sources, width), jnp.float32))
    index = jnp.transpose(jnp.concatenate(halves, axis=0))
    for k in range(sources):
        spread[k * data:(k + 1) * data, :] = moved_ref[k, :data, :].astype(jnp.float32)
    total = sources * docs
    for block in range(2):
        where = []
        for slot in range(2):
            lane = block * 2 + slot
            where.append(jnp.concatenate(
                [jnp.broadcast_to(index[lane * docs:(lane + 1) * docs, k:k + 1], (docs, width))
                 for k in range(sources)], axis=0))
        first = spread[pl.ds(block * 2, total, stride=group), :]
        second = spread[pl.ds(block * 2 + 1, total, stride=group), :]
        first = jnp.where(where[0] == where[1], first + second, first)
        values[block * 2] = first.astype(jnp.bfloat16)
        values[block * 2 + 1] = second.astype(jnp.bfloat16)
        tiles[block * 2] = where[0].astype(jnp.bfloat16)
        tiles[block * 2 + 1] = where[1].astype(jnp.bfloat16)

    core = core_ref[0]
    tiles_step = depth // width

    out_ref[...] = jnp.zeros_like(out_ref)

    @pl.loop(0, 2 * STEPS)
    def _(step):
        block = jnp.where(step < STEPS, core, 1 - core)
        base = (lax.rem(step, STEPS) * tiles_step).astype(jnp.float32)
        total = out_ref[...]
        for chunk in range(tiles_step // 2):
            k = step * 2 + chunk // (tiles_step // 4)
            if chunk % (tiles_step // 4) == 0:
                pltpu.make_async_copy(own_ref.at[pl.ds(0, unit)], weights.at[k], sems.at[k]).wait()

                @pl.when(k + AHEAD < units // 2)
                def _():
                    fetch(own_ref, k + AHEAD)

                @pl.when(jnp.logical_and(k + AHEAD >= units // 2, k + AHEAD < units))
                def _():
                    fetch(other_ref, k + AHEAD)

            parts = []
            for t in (2 * chunk, 2 * chunk + 1):
                mark = jnp.full((1, width), base + t, jnp.float32).astype(jnp.bfloat16)
                parts.append(jnp.where(
                    tiles[block * 2] == mark, values[block * 2],
                    jnp.where(tiles[block * 2 + 1] == mark, values[block * 2 + 1], jnp.zeros((), jnp.bfloat16))))
            dense = jnp.concatenate(parts, axis=1)
            total = total + jnp.dot(
                dense, weights[k, 2 * chunk * width % unit:2 * chunk * width % unit + 2 * width, :],
                preferred_element_type=jnp.float32)
        out_ref[...] = total


def combine_kernel(scale, made_a, got_a, made_b, got_b, early_ref, out_ref):
    share = made_a.shape[0]
    out_ref[:share, :] = (made_a[...] + got_a[...]) * scale - early_ref[:share, :]
    out_ref[share:, :] = (made_b[...] + got_b[...]) * scale - early_ref[share:, :]


def to_half(values, scale):
    return (values * scale).astype(jnp.float16)


def from_half(values, scale):
    return values.astype(jnp.float32) * (1.0 / scale)


def shards(counts, tile_index, tile_count, whitening, factors):
    doc_axes = ('c', 'x', 'zh')
    doc_devices = lax.axis_size(doc_axes)
    chips = doc_devices // 2
    doc_local = counts.shape[0]
    slots = counts.shape[1] // doc_devices
    width = counts.shape[2]
    topics = whitening.shape[1]
    half = doc_local * chips
    group = 2 * slots
    swap = [(0, 1), (1, 0)]
    vmem = pl.BlockSpec(memory_space=pltpu.VMEM)
    anywhere = pl.BlockSpec(memory_space=pl.ANY)

    other = lax.ppermute(whitening, "c", swap)
    units = doc_local // 2 + 2
    packed = pl.pallas_call(
        pack_kernel,
        out_shape=jax.ShapeDtypeStruct((doc_devices, units, group, width), jnp.bfloat16),
        in_specs=[anywhere, anywhere, anywhere],
        out_specs=anywhere,
        scratch_shapes=[
            pltpu.VMEM(tile_index.shape[::-1], tile_index.dtype),
            pltpu.VMEM(tile_count.shape[::-1], tile_count.dtype),
            pltpu.VMEM((doc_devices, units, group, width), jnp.bfloat16),
            pltpu.SemaphoreType.DMA((2,)),
            pltpu.SemaphoreType.DMA((doc_devices,)),
            pltpu.SemaphoreType.DMA((doc_devices,)),
        ],
        compiler_params=pltpu.CompilerParams(vmem_limit_bytes=61 << 20),
        cost_estimate=pl.CostEstimate(flops=1 << 20, bytes_accessed=2 << 20, transcendentals=0),
        name="pack",
    )(tile_index.T, tile_count.T, counts.reshape(doc_local, chips, group, width))
    moved = lax.all_to_all(packed, doc_axes, 0, 0, tiled=True)
    moved = moved.reshape(doc_devices, units * group, width)

    gram_matrix = jnp.dot(factors.T, factors, precision=HIGH) / topics
    early = penalty * jnp.dot(factors, gram_matrix * gram_matrix, precision=HIGH)
    core = lax.axis_index("c")
    depth = whitening.shape[0] // STEPS
    terms = pl.pallas_call(
        project_kernel,
        out_shape=jax.ShapeDtypeStruct((half, topics), jnp.float32),
        in_specs=[pl.BlockSpec(memory_space=pltpu.SMEM), vmem, anywhere, anywhere, anywhere],
        out_specs=vmem,
        scratch_shapes=[
            pltpu.VMEM((4 * STEPS, depth // 2, topics), jnp.bfloat16),
            pltpu.VMEM((half * group, width), jnp.float32),
            pltpu.VMEM((group, half, width), jnp.bfloat16),
            pltpu.VMEM((group, half, width), jnp.bfloat16),
            pltpu.SemaphoreType.DMA((4 * STEPS,)),
        ],
        compiler_params=pltpu.CompilerParams(vmem_limit_bytes=50 << 20),
        cost_estimate=pl.CostEstimate(
            flops=4 * half * whitening.shape[0] * topics, bytes_accessed=12 << 20, transcendentals=0),
        name="project",
    )(core.astype(jnp.int32).reshape(1), moved, whitening, other, early)

    plane_axes, column_axes = ("y", "x"), ("zl", "zh")
    plane = lax.axis_size(plane_axes)
    column = lax.axis_size(column_axes)
    part = half // plane
    sent = to_half(terms, term_scale).reshape(plane, part, topics)
    got = lax.all_to_all(sent, plane_axes, 0, 0, tiled=True)
    plane_sum = jnp.sum(got.astype(jnp.float32), axis=0) * (1.0 / term_scale)
    sent = jnp.broadcast_to(to_half(plane_sum, total_scale)[None], (column, part, topics))
    got = lax.all_to_all(sent, column_axes, 0, 0, tiled=True)
    total = jnp.sum(got.astype(jnp.float32), axis=0) * (1.0 / total_scale)
    sent = jnp.broadcast_to(to_half(total, total_scale)[None], (plane, part, topics))
    got = lax.all_to_all(sent, plane_axes, 0, 0, tiled=True)
    projected = from_half(got.reshape(half, topics), total_scale)

    scores = jnp.dot(projected, factors, precision=HIGH) * (1.0 / math.sqrt(topics))
    squares = scores * scores
    share = topics // 2
    made, got = [], []
    for k in range(2):
        made.append(jnp.dot(projected[:, k * share:(k + 1) * share].T, squares, precision=HIGH))
        got.append(lax.ppermute(made[k], "c", swap))
    return pl.pallas_call(
        functools.partial(combine_kernel, 1.0 / (2 * half)),
        out_shape=jax.ShapeDtypeStruct((topics, topics), jnp.float32),
        in_specs=[vmem] * 5,
        out_specs=vmem,
        compiler_params=pltpu.CompilerParams(vmem_limit_bytes=16 << 20),
        name="combine",
    )(made[0], got[0], made[1], got[1], early)


def solution(mesh):
    fine = Mesh(mesh.devices.reshape(2, 4, 2, 4, 4), ("zh", "x", "c", "zl", "y"))
    doc, vocab = ("zh", "x", "c"), ("zl", "y")
    in_specs = (P(doc, vocab, None), P(doc, vocab), P(doc, vocab), P(doc + vocab, None), P())
    return jax.shard_map(shards, mesh=fine, in_specs=in_specs, out_specs=P(), check_vma=False)
```
